32 devices in a mesh: dp: 8 (over z, x), tensor: 4 (over y, core).
Axes of the slice: x: 2, y: 2, z: 4, core: 2. Of those that a mesh axis runs over, the one named last changes fastest.
Arguments:
- tokens: bfloat16 [2, 1024, 8, 768], P(None, 'tensor', 'dp'), may hold values from -6 to 6
- segment_ids: int32 [2, 8, 1024], P(None, 'dp'), may hold values from 0 to 17, as said below
- valid_mask: int32 [2, 8, 1024], P(None, 'dp'), may hold values from 0 to 1, as said below
- gain_one: float32 [768], replicated, may hold values from 0.5 to 1.5
- shift_one: float32 [768], replicated, may hold values from -1.25 to 1.25
- w_qkv: bfloat16 [768, 3, 768], P(None, None, 'tensor'), may hold values from -0.21875 to 0.21875
- bias_qv: float32 [2, 768], P(None, 'tensor'), may hold values from -1.75 to 1.75
- output_weight: bfloat16 [768, 768], P('tensor'), may hold values from -1.75 to 1.75
- bias_out: float32 [768], replicated, may hold values from -1.25 to 1.25
- gain_two: float32 [768], replicated, may hold values from 0.5 to 1.5
- shift_two: float32 [768], replicated, may hold values from -1.25 to 1.25
- up_weight: bfloat16 [768, 3072], P(None, 'tensor'), may hold values from -0.21875 to 0.21875
- bias_up: float32 [3072], P('tensor'), may hold values from -1.75 to 1.75
- down_weight: bfloat16 [3072, 768], P('tensor'), may hold values from -0.109375 to 0.109375
- bias_down: float32 [768], replicated, may hold values from -1.25 to 1.25
- out_grad: bfloat16 [2, 1024, 8, 768], P(None, 'tensor', 'dp'), may hold values from -6 to 6
Outputs:
- block_out: bfloat16 [2, 1024, 8, 768], P(None, 'tensor', 'dp')
- grad_tokens: float32 [2, 1024, 8, 768], P(None, 'tensor', 'dp')
- grad_gain_one: float32 [768], replicated
- grad_shift_one: float32 [768], replicated
- grad_w_qkv: float32 [768, 3, 768], P('dp', None, 'tensor')
- grad_bias_qv: float32 [2, 768], P(None, 'tensor')
- grad_w_out: float32 [768, 768], P('tensor', 'dp')
- grad_bias_out: float32 [768], replicated
- grad_gain_two: float32 [768], replicated
- grad_shift_two: float32 [768], replicated
- grad_w_up: float32 [768, 3072], P('dp', 'tensor')
- grad_bias_up: float32 [3072], P('tensor')
- grad_w_down: float32 [3072, 768], P('tensor', 'dp')
- grad_bias_down: float32 [768], replicated
The draws below stay inside these ranges and needn't reach their ends.
Inputs may be any that keep to these rules, and one draw needn't show every extreme that they name: `segment_ids`: within a sequence ids never fall; its documents hold 60 to 800 tokens, except the last, which the sequence's end cuts. `valid_mask`: each sequence has ones on a leading run of at least 768 positions and zeros after it.
All inputs are finite; a program needn't handle non-finite values.
Results may differ from the reference program's by a relative error of at most 0.012.
The reference program's roundings to bfloat16 on the way count: a program that leaves them out, or rounds other values in their place, can miss the bound.
Values may be sent and summed in bfloat16 or wider, within the bound.
A program may use at most 128 MiB of HBM per device.

```python
import math
import jax
import jax.numpy as jnp
from jax import lax

D = 768
HEADS = 12
HEAD_DIM = 64
FF = 3072
LEN = 1024
DOC_MIN = 60
DOC_MAX = 800
MICRO = 2
NSEQ = 8


def draw_segment_ids(key, part):
    count = LEN // DOC_MIN + 1
    lengths = jax.random.randint(jax.random.fold_in(key, 11), (MICRO, NSEQ, count), DOC_MIN, DOC_MAX + 1)
    chosen_micro = jax.random.randint(jax.random.fold_in(key, 31), (), 0, MICRO)
    chosen_seq = jax.random.randint(jax.random.fold_in(key, 37), (), 0, NSEQ)
    dense = (jnp.arange(MICRO, dtype=jnp.int32)[:, None, None] == chosen_micro) & (jnp.arange(NSEQ, dtype=jnp.int32)[None, :, None] == chosen_seq)
    lengths = jnp.where(dense, DOC_MIN, lengths)
    ends = jnp.cumsum(lengths, axis=-1)
    place = jnp.arange(LEN, dtype=jnp.int32)
    return jnp.sum((ends[:, :, None, :] <= place[None, None, :, None]).astype(jnp.int32), axis=-1)


def draw_valid_mask(key, part):
    kept = jax.random.randint(jax.random.fold_in(key, 23), (MICRO, NSEQ, 1), LEN - LEN // 4, LEN + 1)
    place = jnp.arange(LEN, dtype=jnp.int32)
    return (place[None, None, :] < kept).astype(jnp.int32)


def block_scale(stream_key, shape, pieces, low, largest):
    level, own = 1.0, jax.random.fold_in(stream_key, 6)
    for axis_at, blocks in pieces:
        steps = jnp.exp(jax.random.uniform(jax.random.fold_in(own, axis_at), (blocks,), jnp.float32, low / len(pieces), largest / len(pieces)))
        level = level * jnp.repeat(steps, shape[axis_at] // blocks).reshape([-1 if axis == axis_at else 1 for axis in range(len(shape))])
    return level


def scatter_about(rng, dims, width, reach, shards=(), kind=jnp.bfloat16):
    entries = jax.random.normal(rng, dims, jnp.float32) * width
    if len(shards) > 0:
        entries = block_scale(rng, dims, shards, -0.22, 0.18) * entries
    return jnp.clip(entries, min=-reach, max=reach).astype(kind)


def setup_inputs(seed: int = 0) -> dict:
    streams_of = jax.random.split(jax.random.key(seed), 17)
    return {
        "tokens": scatter_about(streams_of[0], (MICRO, LEN, NSEQ, D), 1.0, 6.0, ((1, 4), (2, 8))),
        "segment_ids": draw_segment_ids(jax.random.fold_in(streams_of[16], 71), 0),
        "valid_mask": draw_valid_mask(jax.random.fold_in(streams_of[16], 71), 0),
        "gain_one": jnp.clip(1.0 + 0.1 * jax.random.normal(streams_of[3], (D,), jnp.float32), 0.5, 1.5),
        "shift_one": scatter_about(streams_of[4], (D,), 0.2, 1.25, (), jnp.float32),
        "w_qkv": scatter_about(streams_of[5], (D, 3, D), D ** -0.5, 0.21875, ((2, 4),)),
        "bias_qv": scatter_about(streams_of[6], (2, D), 0.3, 1.75, ((1, 4),), jnp.float32),
        "output_weight": scatter_about(streams_of[7], (D, D), (max(1, D // 64)) ** -0.5, 1.75, ((0, 4),)),
        "bias_out": scatter_about(streams_of[8], (D,), 0.2, 1.25, (), jnp.float32),
        "gain_two": jnp.clip(1.0 + 0.1 * jax.random.normal(streams_of[9], (D,), jnp.float32), 0.5, 1.5),
        "shift_two": scatter_about(streams_of[10], (D,), 0.2, 1.25, (), jnp.float32),
        "up_weight": scatter_about(streams_of[11], (D, FF), D ** -0.5, 0.21875, ((1, 4),)),
        "bias_up": scatter_about(streams_of[12], (FF,), 0.3, 1.75, ((0, 4),), jnp.float32),
        "down_weight": scatter_about(streams_of[13], (FF, D), FF ** -0.5, 0.109375, ((0, 4),)),
        "bias_down": scatter_about(streams_of[14], (D,), 0.2, 1.25, (), jnp.float32),
        "out_grad": scatter_about(streams_of[15], (MICRO, LEN, NSEQ, D), 1.0, 6.0, ((1, 4), (2, 8))),
    }


@jax.custom_vjp
def low(v):
    return lax.optimization_barrier(v.astype(jnp.bfloat16)).astype(jnp.float32)

@jax.custom_vjp
def low_back(v):
    return v

def low_keep(v):
    return (low(v), None)

def low_pass(kept, grad):
    return (grad,)

def back_keep(v):
    return (v, None)

def back_low(kept, grad):
    return (low(grad),)
low.defvjp(low_keep, low_pass)
low_back.defvjp(back_keep, back_low)
eps_norm = 1e-06
masked_score = -1e+30
highest = lax.Precision.HIGHEST

def layer_norm(rows, gain, shift):
    mean = lax.optimization_barrier(jnp.mean(rows, axis=-1, keepdims=True))
    centred = rows - mean
    spread = lax.optimization_barrier(jnp.mean(centred * centred, axis=-1, keepdims=True))
    return centred * lax.rsqrt(spread + eps_norm) * gain + shift

def split_heads(values):
    return values.reshape(values.shape[0], values.shape[1], HEADS, HEAD_DIM)

def forward(params, rows, seg, valid):
    gain_one, shift_one, w_qkv, bias_qv, output_weight, bias_out, gain_two, shift_two, up_weight, bias_up, down_weight, bias_down = params
    group = rows.shape[0]
    normed = low(layer_norm(rows, gain_one, shift_one))
    joined = jnp.einsum('gld,dce->glce', normed, w_qkv, precision=highest)
    queries = low(low_back(joined[:, :, 0] + bias_qv[0]))
    keys_all = low(low_back(joined[:, :, 1]))
    values_all = low(low_back(joined[:, :, 2] + bias_qv[1]))
    scores = jnp.einsum('gqhd,gkhd->ghqk', split_heads(queries), split_heads(keys_all), precision=highest)
    scores = low_back(scores * HEAD_DIM ** (-0.5))
    same = (seg[:, :, None] == seg[:, None, :]) & (valid[:, None, :] > 0)
    allowed = same | jnp.eye(LEN, dtype=bool)[None]
    scores = jnp.where(allowed[:, None], scores, masked_score)
    probs = low(jax.nn.softmax(scores, axis=-1))
    mixed = jnp.einsum('ghqk,gkhd->gqhd', probs, split_heads(values_all), precision=highest)
    mixed = low(low_back(mixed.reshape(group, LEN, D)))
    attn = low_back(jnp.einsum('gle,ef->glf', mixed, output_weight, precision=highest) + bias_out)
    middle = rows + attn
    normed_two = low(layer_norm(middle, gain_two, shift_two))
    upper = low_back(jnp.einsum('gld,df->glf', normed_two, up_weight, precision=highest) + bias_up)
    hidden = low(jax.nn.gelu(upper, approximate=True))
    return middle + jnp.einsum('glf,fd->gld', hidden, down_weight, precision=highest) + bias_down

def reference(tokens, segment_ids, valid_mask, gain_one, shift_one, w_qkv, bias_qv, output_weight, bias_out, gain_two, shift_two, up_weight, bias_up, down_weight, bias_down, out_grad):
    total = MICRO * NSEQ
    group = math.gcd(total, max(1, 4096 // LEN))

    def sequences(values):
        return values.astype(jnp.float32).transpose(0, 2, 1, 3).reshape(total // group, group, LEN, D)
    rows_all = sequences(tokens)
    grads_all = sequences(out_grad)
    seg_all = segment_ids.reshape(total // group, group, LEN)
    valid_all = valid_mask.reshape(total // group, group, LEN)
    params = tuple((p.astype(jnp.float32) for p in (gain_one, shift_one, w_qkv, bias_qv, output_weight, bias_out, gain_two, shift_two, up_weight, bias_up, down_weight, bias_down)))

    def step(acc, item):
        rows, cotangent, seg, valid = item

        def local_forward(weights, inputs):
            return forward(weights, inputs, seg, valid)
        outputs, pullback = jax.vjp(local_forward, params, rows)
        grads, grad_rows = pullback(cotangent)
        acc = jax.tree.map(jnp.add, acc, grads)
        return (acc, (outputs, grad_rows))
    zeros = jax.tree.map(jnp.zeros_like, params)
    acc, (outputs, grad_rows) = lax.scan(step, zeros, (rows_all, grads_all, seg_all, valid_all))

    def restore(values):
        return values.reshape(MICRO, NSEQ, LEN, D).transpose(0, 2, 1, 3)
    return (restore(outputs).astype(jnp.bfloat16), restore(grad_rows), acc[0], acc[1], acc[2], acc[3], acc[4], acc[5], acc[6], acc[7], acc[8], acc[9], acc[10], acc[11])
```

```python
import functools

import jax
import jax.numpy as jnp
from jax import lax
from jax.experimental import pallas as pl
from jax.experimental.pallas import tpu as pltpu
from jax.sharding import PartitionSpec as P

HEAD_DIM = 64
EPS = 1e-06
MASKED = -1e30
SELF_CODE = 4096.0
F32 = jnp.float32
BF16 = jnp.bfloat16
MESH = pl.DeviceIdType.MESH
GELU_A = 0.7978845608028654
GELU_B = 0.044715


def mm(a, b):
    return lax.dot_general(a, b, (((1,), (0,)), ((), ())), preferred_element_type=F32)


def mm_nt(a, b):
    return lax.dot_general(a, b, (((1,), (1,)), ((), ())), preferred_element_type=F32)


def mm_tn(a, b):
    return lax.dot_general(a, b, (((0,), (0,)), ((), ())), preferred_element_type=F32)


def mm_tt(a, b):
    return lax.dot_general(a, b, (((0,), (1,)), ((), ())), preferred_element_type=F32)


def norm_parts(v):
    mean = jnp.mean(v, axis=-1, keepdims=True)
    cen = v - mean
    r = lax.rsqrt(jnp.mean(cen * cen, axis=-1, keepdims=True) + EPS)
    return cen * r, r


def norm_back(e, n, r):
    first = jnp.mean(e, axis=-1, keepdims=True)
    second = jnp.mean(e * n, axis=-1, keepdims=True)
    return r * (e - first - n * second)


class Names:
    def __init__(self, send, recv):
        self.send, self.recv, self.used = send, recv, 0

    def copy(self, src, dst, device):
        i = self.used
        self.used += 1
        return pltpu.make_async_remote_copy(
            src_ref=src,
            dst_ref=dst,
            send_sem=self.send.at[i],
            recv_sem=self.recv.at[i],
            device_id=device,
            device_id_type=MESH,
        )


SEMS = 120


def block_kernel(
    n_dp,
    in_dp,
    x_ref,
    g_ref,
    seg_ref,
    val_ref,
    gain1,
    shift1,
    bias_qv,
    bias_out,
    gain2,
    shift2,
    bias_up,
    bias_down,
    wqkv_hbm,
    wo_hbm,
    wu_hbm,
    wd_hbm,
    out_ref,
    gtok_ref,
    small_ref,
    qvb_ref,
    own_a,
    own_b,
    wq,
    wo,
    wu,
    wd,
    a_all,
    c_all,
    g_all,
    d_all,
    qT,
    kT,
    vT,
    kk,
    vv,
    oT,
    lse,
    doT,
    h_scr,
    du_scr,
    kcol,
    bias_scr,
    s_scr,
    p_scr,
    ds_scr,
    dkT,
    dvT,
    dqkvT,
    part,
    crecv,
    ysend,
    yrecv,
    mid,
    ga,
    gb,
    *rest,
):
    if in_dp:
        xs_a, xr_a, zr_a, xs_b, xr_b, zr_b, vec, trecv, dsend, drecv, send_sem, recv_sem, w_sem = rest
    else:
        vec, send_sem, recv_sem, w_sem = rest
    micro, R, D = x_ref.shape
    L = 4 * R
    HL = wo.shape[0]
    FL = wu.shape[1]
    heads = HL // HEAD_DIM
    scale = HEAD_DIM ** (-0.5)
    t = lax.axis_index("tensor")
    dp = lax.axis_index("dp")
    t_core = t + 1 - 2 * lax.rem(t, 2)
    t_y = lax.rem(t + 2, 4)
    t_diag = t_core + 2 - 4 * (t_core // 2)
    blocks = (t, t_core, t_y, t_diag)
    core = {"tensor": t_core}
    ydev = {"tensor": t_y}
    names = Names(send_sem, recv_sem)

    barrier = pltpu.get_barrier_semaphore()
    met = 0
    for dev in (t_core, t_y, t_diag):
        pl.semaphore_signal(barrier, inc=1, device_id={"tensor": dev}, device_id_type=MESH)
        met += 1
    if in_dp:
        for off in range(1, n_dp):
            pl.semaphore_signal(barrier, inc=1, device_id={"dp": lax.rem(dp + off, n_dp)}, device_id_type=MESH)
            met += 1
    loads = [
        pltpu.make_async_copy(s, d, w_sem.at[i])
        for i, (s, d) in enumerate(((wqkv_hbm, wq), (wo_hbm, wo), (wu_hbm, wu), (wd_hbm, wd)))
    ]
    for ld in loads:
        ld.start()

    CH = min(64, R)
    KC = min(128, R)

    half = R // 2

    class Gather:
        def __init__(self, buf, m):
            b = self.b = buf
            self.core = names.copy(b.at[m, 0], b.at[m, 1], core)
            self.y = [names.copy(b.at[m, 0, pl.ds(i * half, half)], b.at[m, 2, pl.ds(i * half, half)], ydev) for i in range(2)]
            self.fwd = [names.copy(b.at[m, 2, pl.ds(i * half, half)], b.at[m, 3, pl.ds(i * half, half)], core) for i in range(2)]

        def start_core(self):
            self.core.start()

        def start_y(self):
            for c in self.y:
                c.start()

        def wait_core(self):
            self.core.wait_recv()

        def forward(self):
            for c, f in zip(self.y, self.fwd):
                c.wait_recv()
                f.start()

        def wait_last(self):
            for f in self.fwd:
                f.wait_recv()

        def drain(self):
            for c in [self.core] + self.y + self.fwd:
                c.wait_send()

    class Scatter:
        def __init__(self, p):
            self.p = p
            self.c3 = names.copy(part.at[p, 3], crecv.at[p, 1], core)
            self.c1 = names.copy(part.at[p, 1], crecv.at[p, 0], core)
            self.y = names.copy(ysend.at[p], yrecv.at[p], ydev)

        def start_far(self):
            self.c3.start()

        def start_near(self):
            self.c1.start()

        def relay(self):
            p = self.p
            self.c3.wait_recv()

            @pl.loop(0, R // CH)
            def _(i):
                rows = pl.ds(pl.multiple_of(i * CH, CH), CH)
                ysend[p, rows, :] = (part[p, 2, rows, :].astype(F32) + crecv[p, 1, rows, :].astype(F32)).astype(BF16)

            self.y.start()

        def arrive(self):
            self.c1.wait_recv()
            self.y.wait_recv()

        def total(self, rows):
            p = self.p
            return part[p, 0, rows, :].astype(F32) + crecv[p, 0, rows, :].astype(F32) + yrecv[p, rows, :].astype(F32)

        def drain(self):
            for c in (self.c3, self.c1, self.y):
                c.wait_send()

    def by_rows(step):
        @pl.loop(0, R // CH)
        def _(i):
            step(pl.ds(pl.multiple_of(i * CH, CH), CH))

    ag_a = [Gather(a_all, m) for m in range(micro)]
    ag_c = [Gather(c_all, m) for m in range(micro)]
    ag_g = [Gather(g_all, m) for m in range(micro)]
    ag_d = [Gather(d_all, m) for m in range(micro)]
    rs_attn = [Scatter(m) for m in range(micro)]
    rs_branch = [Scatter(m) for m in range(micro)]
    rs_dc = [Scatter(micro + m) for m in range(micro)]
    rs_da = [Scatter(micro + m) for m in range(micro)]

    def first_norm(m):
        def step(rows):
            n, _ = norm_parts(x_ref[m, rows, :].astype(F32))
            a_all[m, 0, rows, :] = (n * gain1[...] + shift1[...]).astype(BF16)

        by_rows(step)

    def codes(m):
        for r in range(4):
            seg = seg_ref[pl.ds(m, 1), pl.ds(pl.multiple_of(blocks[r] * R, R), R)].astype(F32)
            val = val_ref[pl.ds(m, 1), pl.ds(pl.multiple_of(blocks[r] * R, R), R)]
            place = lax.broadcasted_iota(jnp.int32, (1, R), 1).astype(F32) + (SELF_CODE + r * R)
            code = jnp.where(val > 0, seg, place)
            kcol[pl.ds(r * R, R), :] = jnp.broadcast_to(code, (128, R)).T

    def qkv(m):
        def slot(r):
            a = a_all[m, r]
            cols = slice(r * R, (r + 1) * R)
            allT = mm_nt(wq[...], a)
            bq = bias_qv[0].reshape(HL, 1)
            bv = bias_qv[1].reshape(HL, 1)
            q_low = (allT[:HL] + bq).astype(BF16)
            qT[m, :, cols] = q_low * jnp.asarray(scale, BF16)
            kT[m, :, cols] = allT[HL : 2 * HL].astype(BF16)
            vT[m, :, cols] = (allT[2 * HL :] + bv).astype(BF16)
            kv = mm_nt(a, wq[HL:, :])
            for h in range(heads):
                kk[m, h, cols, :] = kv[:, h * HEAD_DIM : (h + 1) * HEAD_DIM].astype(BF16)
                bv_row = jnp.broadcast_to(bv, (HL, 128)).T[:1, h * HEAD_DIM : (h + 1) * HEAD_DIM]
                vv[m, h, cols, :] = (kv[:, HL + h * HEAD_DIM : HL + (h + 1) * HEAD_DIM] + bv_row).astype(BF16)

        slot(0)
        ag_a[m].wait_core()
        slot(1)
        ag_a[m].forward()
        slot(2)
        ag_a[m].wait_last()
        slot(3)

    def mask_block(m, qb):
        cols = pl.ds(pl.multiple_of(qb * R, R), R)
        place = (lax.broadcasted_iota(jnp.int32, (1, R), 1) + qb * R).astype(F32) + SELF_CODE
        blk = jnp.where(qb == 0, blocks[0], jnp.where(qb == 1, blocks[1], jnp.where(qb == 2, blocks[2], blocks[3])))
        seg = seg_ref[pl.ds(m, 1), pl.ds(pl.multiple_of(blk * R, R), R)].astype(F32)
        for c in range(L // KC):
            kc = kcol[c * KC : (c + 1) * KC, :1]
            ok = (kc == seg) | (kc == place)
            bias_scr[c * KC : (c + 1) * KC, :] = jnp.where(ok, 0.0, MASKED)
        return cols

    def fold8(v, op):
        out = v[:8]
        for i in range(1, v.shape[0] // 8):
            out = op(out, v[i * 8 : (i + 1) * 8])
        return out

    def attend(m):
        @pl.loop(0, 4)
        def _(qb):
            cols = mask_block(m, qb)

            @pl.loop(0, heads)
            def _(h):
                hrows = pl.ds(pl.multiple_of(h * HEAD_DIM, HEAD_DIM), HEAD_DIM)
                q = qT[m, hrows, cols]
                top8 = None
                for c in range(L // KC):
                    rows = slice(c * KC, (c + 1) * KC)
                    s = mm(kk[m, h, rows, :], q) + bias_scr[rows, :]
                    s_scr[rows, :] = s
                    part8 = fold8(s, jnp.maximum)
                    top8 = part8 if top8 is None else jnp.maximum(top8, part8)
                top = jnp.max(top8, axis=0, keepdims=True)
                sum8 = None
                for c in range(L // KC):
                    rows = slice(c * KC, (c + 1) * KC)
                    p = jnp.exp(s_scr[rows, :] - top)
                    p_scr[rows, :] = p.astype(BF16)
                    part8 = fold8(p, jnp.add)
                    sum8 = part8 if sum8 is None else sum8 + part8
                total = jnp.sum(sum8, axis=0, keepdims=True)
                o = mm(vT[m, hrows, :], p_scr[...])
                oT[m, hrows, cols] = (o / total).astype(BF16)
                lse[m, pl.ds(h, 1), cols] = top + jnp.log(total)

    def attn_out(m):
        rs = rs_attn[m]
        for r in (3, 2, 1, 0):
            part[m, r] = mm_tn(oT[m, :, r * R : (r + 1) * R], wo[...]).astype(BF16)
            if r == 3:
                rs.start_far()
            if r == 1:
                rs.start_near()
                rs.relay()

    def middle(m):
        rs_attn[m].arrive()

        def step(rows):
            v = x_ref[m, rows, :].astype(F32) + (rs_attn[m].total(rows) + bias_out[...])
            mid[m, rows, :] = v
            n, _ = norm_parts(v)
            c_all[m, 0, rows, :] = (n * gain2[...] + shift2[...]).astype(BF16)

        by_rows(step)
        ag_c[m].start_core()
        ag_c[m].start_y()

    def feed(m, first):
        @pl.loop(first, first + 2)
        def _(r):
            rows = pl.ds(pl.multiple_of(r * R, R), R)
            g = g_all[m, r]
            u = mm(c_all[m, r], wu[...]) + bias_up[...]
            dh = mm_nt(g, wd[...])
            th = jnp.tanh(GELU_A * (u + GELU_B * (u * u * u)))
            half_u = 0.5 * (1.0 + th)
            slope = half_u + (0.5 * u) * (1.0 - th * th) * (GELU_A * (1.0 + (3.0 * GELU_B) * (u * u)))
            hid = (u * half_u).astype(BF16)
            du = (dh * slope).astype(BF16)
            h_scr[rows, :] = hid
            du_scr[rows, :] = du
            vec[6:7, :FL] += jnp.sum(du.astype(F32), axis=0, keepdims=True)
            part[micro + m, r] = mm_nt(du, wu[...]).astype(BF16)
            part[m, r] = mm(hid, wd[...]).astype(BF16)

    def weight_sums(m):
        B = min(256, D)

        @pl.loop(0, D // B)
        def _(i):
            f = pl.ds(pl.multiple_of(i * B, B), B)
            for r in range(4):
                down = mm_tn(g_all[m, r, :, f], h_scr[r * R : (r + 1) * R, :])
                up = mm_tn(c_all[m, r, :, f], du_scr[r * R : (r + 1) * R, :])
                if m == 0 and r == 0:
                    ga[f, :FL] = down
                    ga[f, FL:] = up
                else:
                    ga[f, :FL] += down
                    ga[f, FL:] += up

    def add_row(i, v):
        vec[i : i + 1, :] += jnp.sum(v, axis=0, keepdims=True)

    def turn(m):
        rs_dc[m].arrive()

        def step(rows):
            dc = rs_dc[m].total(rows)
            n, r = norm_parts(mid[m, rows, :])
            add_row(3, dc * n)
            add_row(4, dc)
            g = g_ref[m, rows, :].astype(F32)
            add_row(5, g)
            dx = g + norm_back(dc * gain2[...], n, r)
            gtok_ref[m, rows, :] = dx
            low = dx.astype(BF16)
            add_row(2, low.astype(F32))
            d_all[m, 0, rows, :] = low

        by_rows(step)
        ag_d[m].start_core()
        ag_d[m].start_y()

    def attend_back(m):
        def project(r):
            doT[:, r * R : (r + 1) * R] = mm_nt(wo[...], d_all[m, r]).astype(BF16)

        project(0)
        ag_d[m].wait_core()
        project(1)
        ag_d[m].forward()
        project(2)
        ag_d[m].wait_last()
        project(3)
        dkT[...] = jnp.zeros_like(dkT)
        dvT[...] = jnp.zeros_like(dvT)

        @pl.loop(0, 4)
        def _(qb):
            cols = mask_block(m, qb)

            @pl.loop(0, heads)
            def _(h):
                hrows = pl.ds(pl.multiple_of(h * HEAD_DIM, HEAD_DIM), HEAD_DIM)
                q = qT[m, hrows, cols]
                do = doT[hrows, cols]
                inner = jnp.sum(do.astype(F32) * oT[m, hrows, cols].astype(F32), axis=0, keepdims=True)
                log_total = lse[m, pl.ds(h, 1), cols]
                for c in range(L // KC):
                    rows = slice(c * KC, (c + 1) * KC)
                    s = mm(kk[m, h, rows, :], q) + bias_scr[rows, :]
                    p = jnp.exp(s - log_total)
                    dprob = mm(vv[m, h, rows, :], do)
                    p_scr[rows, :] = p.astype(BF16)
                    ds_scr[rows, :] = (p * (dprob - inner)).astype(BF16)
                dvT[hrows, :] += mm_nt(do, p_scr[...])
                dkT[hrows, :] += mm_nt(q, ds_scr[...])
                dqkvT[hrows, cols] = (mm(kT[m, hrows, :], ds_scr[...]) * scale).astype(BF16)

        dqkvT[HL : 2 * HL, :] = dkT[...].astype(BF16)
        dqkvT[2 * HL :, :] = dvT[...].astype(BF16)
        rs = rs_da[m]
        for r in (3, 2, 1, 0):
            part[micro + m, r] = mm_tn(dqkvT[:, r * R : (r + 1) * R], wq[...]).astype(BF16)
            if r == 3:
                rs.start_far()
            if r == 1:
                rs.start_near()
                rs.relay()

    def head_sums(m):
        B = min(256, D)
        sums = mm_nt(jnp.ones((8, L), BF16), dqkvT[...])[:1]
        if m == 0:
            qvb_ref[...] = sums
        else:
            qvb_ref[...] += sums

        @pl.loop(0, D // B)
        def _(i):
            f = pl.ds(pl.multiple_of(i * B, B), B)
            for r in range(4):
                cols = slice(r * R, (r + 1) * R)
                j = mm_tt(a_all[m, r, :, f], dqkvT[:, cols])
                o = mm_tt(d_all[m, r, :, f], oT[m, :, cols])
                if m == 0 and r == 0:
                    gb[f, : 3 * HL] = j
                    gb[f, 3 * HL :] = o
                else:
                    gb[f, : 3 * HL] += j
                    gb[f, 3 * HL :] += o

    def finish_out(m):
        rs_branch[m].arrive()

        def step(rows):
            out_ref[m, rows, :] = (mid[m, rows, :] + (rs_branch[m].total(rows) + bias_down[...])).astype(BF16)

        by_rows(step)

    def finish_in(m):
        rs_da[m].arrive()

        def step(rows):
            da = rs_da[m].total(rows)
            n, r = norm_parts(x_ref[m, rows, :].astype(F32))
            add_row(0, da * n)
            add_row(1, da)
            gtok_ref[m, rows, :] += norm_back(da * gain1[...], n, r)

        by_rows(step)

    class Reduce:
        def __init__(self, acc, xs, xr, zr, own):
            self.acc, self.xs, self.xr, self.zr, self.own = acc, xs, xr, zr, own
            self.rows = D // n_dp
            self.n2 = n_dp // 2
            self.px = lax.rem(dp, 2)
            self.pz = dp // 2
            self.x = names.copy(xs, xr, {"dp": dp + 1 - 2 * self.px})
            self.z = []
            for off in range(1, self.n2):
                to = lax.rem(self.pz + off, self.n2)
                self.z.append(names.copy(xs.at[off - 1], zr.at[off - 1], {"dp": 2 * to + self.px}))

        def at(self, z, px):
            n = self.rows
            return pl.ds(pl.multiple_of((2 * z + px) * n, n), n)

        def start(self):
            for z in range(self.n2):
                self.xs[z] = self.acc[self.at(z, 1 - self.px), :].astype(BF16)
            self.x.start()

        def second(self):
            self.x.wait_send()
            self.x.wait_recv()
            for off in range(1, self.n2):
                to = lax.rem(self.pz + off, self.n2)
                self.xs[off - 1] = (self.acc[self.at(to, self.px), :] + self.xr[to].astype(F32)).astype(BF16)
                self.z[off - 1].start()

        def last(self):
            tot = self.acc[self.at(self.pz, self.px), :] + self.xr[self.pz].astype(F32)
            for off in range(1, self.n2):
                self.z[off - 1].wait_recv()
                tot = tot + self.zr[off - 1].astype(F32)
            self.own[...] = tot

        def drain(self):
            for c in self.z:
                c.wait_send()

    if in_dp:
        red_a = Reduce(ga, xs_a, xr_a, zr_a, own_a)
        red_b = Reduce(gb, xs_b, xr_b, zr_b, own_b)
        small_t = [names.copy(vec, trecv.at[i], {"tensor": d}) for i, d in enumerate((t_core, t_y, t_diag))]
        small_d = [names.copy(dsend, drecv.at[off - 1], {"dp": lax.rem(dp + off, n_dp)}) for off in range(1, n_dp)]

    vec[...] = jnp.zeros_like(vec)
    for m in range(micro):
        g_all[m, 0] = g_ref[m]
    first_norm(0)
    pl.semaphore_wait(barrier, met)
    ag_a[0].start_core()
    ag_a[0].start_y()
    for m in range(1, micro):
        first_norm(m)
        ag_a[m].start_core()
        ag_a[m].start_y()
    for m in range(micro):
        ag_g[m].start_core()
    ag_g[0].start_y()
    codes(0)
    loads[0].wait()
    loads[1].wait()

    qkv(0)
    attend(0)
    attn_out(0)
    codes(1)
    qkv(1)
    attend(1)
    middle(0)
    attn_out(1)
    ag_g[1].start_y()
    loads[2].wait()
    loads[3].wait()

    def feed_all(m, between):
        ag_c[m].wait_core()
        ag_g[m].wait_core()
        rs_attn[m].drain()
        feed(m, 0)
        between()
        ag_c[m].forward()
        ag_g[m].forward()
        ag_c[m].wait_last()
        ag_g[m].wait_last()
        feed(m, 2)
        rs_dc[m].start_far()
        rs_dc[m].start_near()
        rs_dc[m].relay()
        rs_branch[m].start_far()
        rs_branch[m].start_near()
        rs_branch[m].relay()
        weight_sums(m)

    feed_all(0, lambda: middle(1))
    feed_all(1, lambda: turn(0))
    if in_dp:
        red_a.start()
    turn(1)
    codes(0)
    rs_dc[0].drain()
    attend_back(0)
    head_sums(0)
    finish_out(0)
    finish_out(1)
    if in_dp:
        red_a.second()
    codes(1)
    rs_dc[1].drain()
    attend_back(1)
    head_sums(1)
    if in_dp:
        red_b.start()
        red_a.last()
    finish_in(0)
    finish_in(1)
    if in_dp:
        red_b.second()
        vec[7:8, : 3 * HL] = qvb_ref[...]
        for c in small_t:
            c.start()
        for c in small_t:
            c.wait_recv()
        six = lax.broadcasted_iota(jnp.int32, vec.shape, 0) < 6
        dsend[...] = vec[...] + jnp.where(six, trecv[0] + trecv[1] + trecv[2], 0.0)
        for c in small_d:
            c.start()
        red_b.last()
        tot = dsend[...]
        for i, c in enumerate(small_d):
            c.wait_recv()
            tot = tot + drecv[i]
        small_ref[...] = tot
        for c in small_t + small_d:
            c.wait_send()
        red_a.drain()
        red_b.drain()
    else:
        small_ref[...] = vec[...]
        own_a[...] = ga[...]
        own_b[...] = gb[...]
    for m in range(micro):
        rs_branch[m].drain()
        rs_da[m].drain()
        for gather in (ag_a, ag_c, ag_g, ag_d):
            gather[m].drain()


def body(
    n_dp,
    tokens,
    segment_ids,
    valid_mask,
    gain_one,
    shift_one,
    w_qkv,
    bias_qv,
    output_weight,
    bias_out,
    gain_two,
    shift_two,
    up_weight,
    bias_up,
    down_weight,
    bias_down,
    out_grad,
):
    micro, R, _, D = tokens.shape
    L = 4 * R
    HL = w_qkv.shape[2]
    FL = up_weight.shape[1]
    heads = HL // HEAD_DIM
    in_dp = n_dp > 1 and n_dp % 2 == 0 and D % n_dp == 0 and (D // n_dp) % 16 == 0
    n2, rows = n_dp // 2, D // n_dp
    row = lambda v: v.reshape(1, -1)
    wqT = jnp.transpose(w_qkv, (1, 2, 0)).reshape(3 * HL, D)
    vmem = pl.BlockSpec(memory_space=pltpu.VMEM)
    hbm = pl.BlockSpec(memory_space=pl.ANY)
    own_rows = rows if in_dp else D
    ca, cb = 2 * FL, 4 * HL
    scratch = [
        pltpu.VMEM((3 * HL, D), BF16),
        pltpu.VMEM((HL, D), BF16),
        pltpu.VMEM((D, FL), BF16),
        pltpu.VMEM((FL, D), BF16),
        pltpu.VMEM((micro, 4, R, D), BF16),
        pltpu.VMEM((micro, 4, R, D), BF16),
        pltpu.VMEM((micro, 4, R, D), BF16),
        pltpu.VMEM((micro, 4, R, D), BF16),
        pltpu.VMEM((micro, HL, L), BF16),
        pltpu.VMEM((micro, HL, L), BF16),
        pltpu.VMEM((micro, HL, L), BF16),
        pltpu.VMEM((micro, heads, L, HEAD_DIM), BF16),
        pltpu.VMEM((micro, heads, L, HEAD_DIM), BF16),
        pltpu.VMEM((micro, HL, L), BF16),
        pltpu.VMEM((micro, heads, L), F32),
        pltpu.VMEM((HL, L), BF16),
        pltpu.VMEM((L, FL), BF16),
        pltpu.VMEM((L, FL), BF16),
        pltpu.VMEM((L, 128), F32),
        pltpu.VMEM((L, R), F32),
        pltpu.VMEM((L, R), F32),
        pltpu.VMEM((L, R), BF16),
        pltpu.VMEM((L, R), BF16),
        pltpu.VMEM((HL, L), F32),
        pltpu.VMEM((HL, L), F32),
        pltpu.VMEM((3 * HL, L), BF16),
        pltpu.VMEM((2 * micro, 4, R, D), BF16),
        pltpu.VMEM((2 * micro, 2, R, D), BF16),
        pltpu.VMEM((2 * micro, R, D), BF16),
        pltpu.VMEM((2 * micro, R, D), BF16),
        pltpu.VMEM((micro, R, D), F32),
        pltpu.VMEM((D, ca), F32),
        pltpu.VMEM((D, cb), F32),
    ]
    if in_dp:
        for c in (ca, cb):
            scratch += [
                pltpu.VMEM((n2, rows, c), BF16),
                pltpu.VMEM((n2, rows, c), BF16),
                pltpu.VMEM((n2 - 1, rows, c), BF16),
            ]
    scratch += [pltpu.VMEM((8, D), F32)]
    if in_dp:
        scratch += [pltpu.VMEM((3, 8, D), F32), pltpu.VMEM((8, D), F32), pltpu.VMEM((n_dp - 1, 8, D), F32)]
    scratch += [pltpu.SemaphoreType.DMA((SEMS,)), pltpu.SemaphoreType.DMA((SEMS,)), pltpu.SemaphoreType.DMA((4,))]
    outs = pl.pallas_call(
        functools.partial(block_kernel, n_dp, in_dp),
        out_shape=(
            jax.ShapeDtypeStruct((micro, R, D), BF16),
            jax.ShapeDtypeStruct((micro, R, D), F32),
            jax.ShapeDtypeStruct((8, D), F32),
            jax.ShapeDtypeStruct((1, 3 * HL), F32),
            jax.ShapeDtypeStruct((own_rows, ca), F32),
            jax.ShapeDtypeStruct((own_rows, cb), F32),
        ),
        in_specs=[vmem] * 12 + [hbm] * 4,
        out_specs=[vmem] * 6,
        scratch_shapes=scratch,
        compiler_params=pltpu.CompilerParams(
            collective_id=0, has_side_effects=True, vmem_limit_bytes=67043328
        ),
        name="vision_block",
    )(
        tokens.reshape(micro, R, D),
        out_grad.reshape(micro, R, D),
        segment_ids.reshape(micro, L),
        valid_mask.reshape(micro, L),
        row(gain_one),
        row(shift_one),
        bias_qv.reshape(2, HL, 1),
        row(bias_out),
        row(gain_two),
        row(shift_two),
        row(bias_up),
        row(bias_down),
        wqT,
        output_weight,
        up_weight,
        down_weight,
    )
    out, gtok, small, qvb, share_a, share_b = outs
    if not in_dp:
        share_a, share_b = (lax.psum_scatter(v, "dp", scatter_dimension=0, tiled=True) for v in (share_a, share_b))
        small = jnp.concatenate([lax.psum(small[:6], ("dp", "tensor")), lax.psum(small[6:7], "dp")])
        sums = lax.psum(qvb[0], "dp")
    else:
        sums = small[7, : 3 * HL]
    own_rows = share_a.shape[0]
    grad_qkv = share_b[:, : 3 * HL].reshape(own_rows, 3, HL)
    grad_bias_qv = jnp.stack([sums[:HL], sums[2 * HL :]])
    return (
        out.reshape(micro, R, 1, D),
        gtok.reshape(micro, R, 1, D),
        small[0],
        small[1],
        grad_qkv,
        grad_bias_qv,
        share_b[:, 3 * HL :].T,
        small[2],
        small[3],
        small[4],
        share_a[:, FL:],
        small[6, :FL],
        share_a[:, :FL].T,
        small[5],
    )


def solution(mesh):
    placed = (
        P(None, "tensor", "dp", None),
        P(None, "dp", None),
        P(None, "dp", None),
        P(),
        P(),
        P(None, None, "tensor"),
        P(None, "tensor"),
        P("tensor", None),
        P(),
        P(),
        P(),
        P(None, "tensor"),
        P("tensor"),
        P("tensor", None),
        P(),
        P(None, "tensor", "dp", None),
    )
    return jax.shard_map(
        functools.partial(body, mesh.shape["dp"]),
        mesh=mesh,
        in_specs=placed,
        out_specs=(
            P(None, "tensor", "dp", None),
            P(None, "tensor", "dp", None),
            P(),
            P(),
            P("dp", None, "tensor"),
            P(None, "tensor"),
            P("tensor", "dp"),
            P(),
            P(),
            P(),
            P("dp", "tensor"),
            P("tensor"),
            P("tensor", "dp"),
            P(),
        ),
        check_vma=False,
    )
```

```python
import functools

import jax
import jax.numpy as jnp
from jax import lax
from jax.experimental import pallas as pl
from jax.experimental.pallas import tpu as pltpu
from jax.sharding import PartitionSpec as P

HEAD_DIM = 64
EPS = 1e-06
MASKED = -1e30
SELF_CODE = 4096.0
F32 = jnp.float32
BF16 = jnp.bfloat16
MESH = pl.DeviceIdType.MESH
GELU_A = 0.7978845608028654
GELU_B = 0.044715


def mm(a, b):
    return lax.dot_general(a, b, (((1,), (0,)), ((), ())), preferred_element_type=F32)


def mm_nt(a, b):
    return lax.dot_general(a, b, (((1,), (1,)), ((), ())), preferred_element_type=F32)


def mm_tn(a, b):
    return lax.dot_general(a, b, (((0,), (0,)), ((), ())), preferred_element_type=F32)


def mm_tt(a, b):
    return lax.dot_general(a, b, (((0,), (1,)), ((), ())), preferred_element_type=F32)


def norm_parts(v):
    mean = jnp.mean(v, axis=-1, keepdims=True)
    cen = v - mean
    r = lax.rsqrt(jnp.mean(cen * cen, axis=-1, keepdims=True) + EPS)
    return cen * r, r


def norm_back(e, n, r):
    first = jnp.mean(e, axis=-1, keepdims=True)
    second = jnp.mean(e * n, axis=-1, keepdims=True)
    return r * (e - first - n * second)


class Names:
    def __init__(self, send, recv):
        self.send, self.recv, self.used = send, recv, 0

    def copy(self, src, dst, device):
        i = self.used
        self.used += 1
        return pltpu.make_async_remote_copy(
            src_ref=src,
            dst_ref=dst,
            send_sem=self.send.at[i],
            recv_sem=self.recv.at[i],
            device_id=device,
            device_id_type=MESH,
        )


SEMS = 120


def block_kernel(
    n_dp,
    in_dp,
    x_ref,
    g_ref,
    seg_ref,
    val_ref,
    gain1,
    shift1,
    bias_qv,
    bias_out,
    gain2,
    shift2,
    bias_up,
    bias_down,
    wqkv_hbm,
    wo_hbm,
    wu_hbm,
    wd_hbm,
    out_ref,
    gtok_ref,
    small_ref,
    qvb_ref,
    own_dn,
    own_up,
    own_o,
    own_j,
    wq,
    wkv,
    wo,
    wu,
    wd,
    a_all,
    c_all,
    g_all,
    d_all,
    qT,
    kT,
    vT,
    kv,
    oT,
    lse,
    doT,
    h_scr,
    du_scr,
    kcol,
    bias_scr,
    s_scr,
    p_scr,
    ds_scr,
    dkT,
    dvT,
    dqkvT,
    part,
    crecv,
    ysend,
    yrecv,
    mid,
    g_dn,
    g_up,
    g_o,
    g_j,
    *rest,
):
    if in_dp:
        stages, (vec, trecv, dsend, drecv, send_sem, recv_sem, w_sem) = rest[:12], rest[12:]
    else:
        vec, send_sem, recv_sem, w_sem = rest
    micro, R, D = x_ref.shape
    line = lambda ref: ref[...].reshape(1, -1)
    L = 4 * R
    HL = wo.shape[0]
    FL = wu.shape[1]
    heads = HL // HEAD_DIM
    scale = HEAD_DIM ** (-0.5)
    t = lax.axis_index("tensor")
    dp = lax.axis_index("dp")
    t_core = t + 1 - 2 * lax.rem(t, 2)
    t_y = lax.rem(t + 2, 4)
    t_diag = t_core + 2 - 4 * (t_core // 2)
    blocks = (t, t_core, t_y, t_diag)
    core = {"tensor": t_core}
    ydev = {"tensor": t_y}
    names = Names(send_sem, recv_sem)

    barrier = pltpu.get_barrier_semaphore()
    met = 0
    for dev in (t_core, t_y, t_diag):
        pl.semaphore_signal(barrier, inc=1, device_id={"tensor": dev}, device_id_type=MESH)
        met += 1
    if in_dp:
        for off in range(1, n_dp):
            pl.semaphore_signal(barrier, inc=1, device_id={"dp": lax.rem(dp + off, n_dp)}, device_id_type=MESH)
            met += 1
    loads = [
        pltpu.make_async_copy(s, d, w_sem.at[i])
        for i, (s, d) in enumerate(((wqkv_hbm, wq), (wo_hbm, wo), (wu_hbm, wu), (wd_hbm, wd)))
    ]
    for h in range(heads):
        for j in range(2):
            src = wqkv_hbm.at[pl.ds((1 + j) * HL + h * HEAD_DIM, HEAD_DIM), :]
            dst = wkv.at[pl.ds((2 * h + j) * HEAD_DIM, HEAD_DIM), :]
            loads.append(pltpu.make_async_copy(src, dst, w_sem.at[len(loads)]))
    for m in range(micro):
        loads.append(pltpu.make_async_copy(g_ref.at[m], g_all.at[m, 0], w_sem.at[len(loads)]))
    for ld in loads:
        ld.start()

    CH = min(64, R)
    KC = min(128, R)

    half = R // 2

    class Gather:
        def __init__(self, buf, m):
            b = self.b = buf
            self.core = names.copy(b.at[m, 0], b.at[m, 1], core)
            self.y = [names.copy(b.at[m, 0, pl.ds(i * half, half)], b.at[m, 2, pl.ds(i * half, half)], ydev) for i in range(2)]
            self.fwd = [names.copy(b.at[m, 2, pl.ds(i * half, half)], b.at[m, 3, pl.ds(i * half, half)], core) for i in range(2)]

        def start_core(self):
            self.core.start()

        def start_y(self):
            for c in self.y:
                c.start()

        def wait_core(self):
            self.core.wait_recv()

        def forward(self):
            for c, f in zip(self.y, self.fwd):
                c.wait_recv()
                f.start()

        def wait_last(self):
            for f in self.fwd:
                f.wait_recv()

        def drain(self):
            for c in [self.core] + self.y + self.fwd:
                c.wait_send()

    class Scatter:
        def __init__(self, p):
            self.p = p
            self.c3 = names.copy(part.at[p, 3], crecv.at[p, 1], core)
            self.c1 = names.copy(part.at[p, 1], crecv.at[p, 0], core)
            self.y = names.copy(ysend.at[p], yrecv.at[p], ydev)

        def start_far(self):
            self.c3.start()

        def start_near(self):
            self.c1.start()

        def relay(self):
            p = self.p
            self.c3.wait_recv()

            @pl.loop(0, R // CH)
            def _(i):
                rows = pl.ds(pl.multiple_of(i * CH, CH), CH)
                ysend[p, rows, :] = (part[p, 2, rows, :].astype(F32) + crecv[p, 1, rows, :].astype(F32)).astype(BF16)

            self.y.start()

        def arrive(self):
            self.c1.wait_recv()
            self.y.wait_recv()

        def total(self, rows):
            p = self.p
            return part[p, 0, rows, :].astype(F32) + crecv[p, 0, rows, :].astype(F32) + yrecv[p, rows, :].astype(F32)

        def drain(self):
            for c in (self.c3, self.c1, self.y):
                c.wait_send()

    def by_rows(step):
        @pl.loop(0, R // CH)
        def _(i):
            step(pl.ds(pl.multiple_of(i * CH, CH), CH))

    ag_a = [Gather(a_all, m) for m in range(micro)]
    ag_c = [Gather(c_all, m) for m in range(micro)]
    ag_g = [Gather(g_all, m) for m in range(micro)]
    ag_d = [Gather(d_all, m) for m in range(micro)]
    rs_attn = [Scatter(m) for m in range(micro)]
    rs_branch = [Scatter(m) for m in range(micro)]
    rs_dc = [Scatter(micro + m) for m in range(micro)]
    rs_da = [Scatter(micro + m) for m in range(micro)]

    def first_norm(m):
        def step(rows):
            n, _ = norm_parts(x_ref[m, rows, :].astype(F32))
            a_all[m, 0, rows, :] = (n * line(gain1) + line(shift1)).astype(BF16)

        by_rows(step)

    def codes(m):
        for r in range(4):
            seg = seg_ref[m, :, pl.ds(pl.multiple_of(blocks[r] * R, R), R)].astype(F32)
            val = val_ref[m, :, pl.ds(pl.multiple_of(blocks[r] * R, R), R)]
            place = lax.broadcasted_iota(jnp.int32, (1, R), 1).astype(F32) + (SELF_CODE + r * R)
            code = jnp.where(val > 0, seg, place)
            kcol[pl.ds(r * R, R), :] = jnp.broadcast_to(code, (128, R)).T

    def qkv(m):
        cols_of = jnp.broadcast_to(bias_qv[...].reshape(2, 1, HL), (2, 8, HL))
        bq = cols_of[0].T[:, :1]
        bv = cols_of[1].T[:, :1]
        none = jnp.zeros((1, HEAD_DIM), F32)
        v_row = bias_qv[1:2, :]
        kv_bias = jnp.concatenate([p for h in range(heads) for p in (none, v_row[:, h * HEAD_DIM : (h + 1) * HEAD_DIM])], axis=1)

        def slot(r):
            a = a_all[m, r]
            cols = slice(r * R, (r + 1) * R)
            allT = mm_nt(wq[...], a)
            qT[m, :, cols] = (allT[:HL] + bq).astype(BF16) * jnp.asarray(scale, BF16)
            kT[m, :, cols] = allT[HL : 2 * HL].astype(BF16)
            vT[m, :, cols] = (allT[2 * HL :] + bv).astype(BF16)
            both = mm_nt(a, wkv[...]) + kv_bias
            for h in range(heads):
                kv[m, h, cols, :] = both[:, h * 128 : (h + 1) * 128].astype(BF16)

        slot(0)
        ag_a[m].wait_core()
        slot(1)
        ag_a[m].forward()
        slot(2)
        ag_a[m].wait_last()
        slot(3)

    def mask_block(m, qb):
        cols = pl.ds(pl.multiple_of(qb * R, R), R)
        place = (lax.broadcasted_iota(jnp.int32, (1, R), 1) + qb * R).astype(F32) + SELF_CODE
        blk = jnp.where(qb == 0, blocks[0], jnp.where(qb == 1, blocks[1], jnp.where(qb == 2, blocks[2], blocks[3])))
        seg = seg_ref[m, :, pl.ds(pl.multiple_of(blk * R, R), R)].astype(F32)
        for c in range(L // KC):
            kc = kcol[c * KC : (c + 1) * KC, :1]
            ok = (kc == seg) | (kc == place)
            bias_scr[c * KC : (c + 1) * KC, :] = jnp.where(ok, 0.0, MASKED)
        return cols

    def fold8(v, op):
        out = v[:8]
        for i in range(1, v.shape[0] // 8):
            out = op(out, v[i * 8 : (i + 1) * 8])
        return out

    def attend(m):
        @pl.loop(0, 4)
        def _(qb):
            cols = mask_block(m, qb)

            @pl.loop(0, heads)
            def _(h):
                hrows = pl.ds(pl.multiple_of(h * HEAD_DIM, HEAD_DIM), HEAD_DIM)
                q = jnp.concatenate([qT[m, hrows, cols], jnp.zeros((HEAD_DIM, R), BF16)], axis=0)
                top8 = None
                for c in range(L // KC):
                    rows = slice(c * KC, (c + 1) * KC)
                    s = mm(kv[m, h, rows, :], q) + bias_scr[rows, :]
                    s_scr[rows, :] = s
                    part8 = fold8(s, jnp.maximum)
                    top8 = part8 if top8 is None else jnp.maximum(top8, part8)
                top = jnp.max(top8, axis=0, keepdims=True)
                sum8 = None
                for c in range(L // KC):
                    rows = slice(c * KC, (c + 1) * KC)
                    p = jnp.exp(s_scr[rows, :] - top)
                    p_scr[rows, :] = p.astype(BF16)
                    part8 = fold8(p, jnp.add)
                    sum8 = part8 if sum8 is None else sum8 + part8
                total = jnp.sum(sum8, axis=0, keepdims=True)
                o = mm(vT[m, hrows, :], p_scr[...])
                oT[m, hrows, cols] = (o / total).astype(BF16)
                lse[m, pl.ds(h, 1), cols] = top + jnp.log(total)

    def attn_out(m):
        rs = rs_attn[m]
        for r in (3, 2, 1, 0):
            part[m, r] = mm_tn(oT[m, :, r * R : (r + 1) * R], wo[...]).astype(BF16)
            if r == 3:
                rs.start_far()
            if r == 1:
                rs.start_near()
                rs.relay()

    def middle(m):
        rs_attn[m].arrive()

        def step(rows):
            v = x_ref[m, rows, :].astype(F32) + (rs_attn[m].total(rows) + line(bias_out))
            mid[m, rows, :] = v
            n, _ = norm_parts(v)
            c_all[m, 0, rows, :] = (n * line(gain2) + line(shift2)).astype(BF16)

        by_rows(step)
        ag_c[m].start_core()
        ag_c[m].start_y()

    def feed(m, first):
        @pl.loop(first, first + 2)
        def _(r):
            rows = pl.ds(pl.multiple_of(r * R, R), R)
            g = g_all[m, r]
            u = mm(c_all[m, r], wu[...]) + line(bias_up)
            dh = mm_nt(g, wd[...])
            th = jnp.tanh(GELU_A * (u + GELU_B * (u * u * u)))
            half_u = 0.5 * (1.0 + th)
            slope = half_u + (0.5 * u) * (1.0 - th * th) * (GELU_A * (1.0 + (3.0 * GELU_B) * (u * u)))
            hid = (u * half_u).astype(BF16)
            du = (dh * slope).astype(BF16)
            h_scr[rows, :] = hid
            du_scr[rows, :] = du
            vec[6:7, :FL] += jnp.sum(du.astype(F32), axis=0, keepdims=True)
            part[micro + m, r] = mm_nt(du, wu[...]).astype(BF16)
            part[m, r] = mm(hid, wd[...]).astype(BF16)

    def weight_sums(m):
        B = min(256, D)

        @pl.loop(0, D // B)
        def _(i):
            f = pl.ds(pl.multiple_of(i * B, B), B)
            for r in range(4):
                down = mm_tn(g_all[m, r, :, f], h_scr[r * R : (r + 1) * R, :])
                up = mm_tn(c_all[m, r, :, f], du_scr[r * R : (r + 1) * R, :])
                if m == 0 and r == 0:
                    g_dn[f, :] = down
                    g_up[f, :] = up
                else:
                    g_dn[f, :] += down
                    g_up[f, :] += up

    def add_row(i, v):
        vec[i : i + 1, :] += jnp.sum(v, axis=0, keepdims=True)

    def turn(m):
        rs_dc[m].arrive()

        def step(rows):
            dc = rs_dc[m].total(rows)
            n, r = norm_parts(mid[m, rows, :])
            add_row(3, dc * n)
            add_row(4, dc)
            g = g_all[m, 0, rows, :].astype(F32)
            add_row(5, g)
            dx = g + norm_back(dc * line(gain2), n, r)
            gtok_ref[m, rows, :] = dx
            low = dx.astype(BF16)
            add_row(2, low.astype(F32))
            d_all[m, 0, rows, :] = low

        by_rows(step)
        ag_d[m].start_core()
        ag_d[m].start_y()

    def attend_back(m, ready, hooks):
        def project(r):
            doT[:, r * R : (r + 1) * R] = mm_nt(wo[...], d_all[m, r]).astype(BF16)

        project(0)
        ag_d[m].wait_core()
        project(1)
        ag_d[m].forward()
        project(2)
        ag_d[m].wait_last()
        project(3)
        ready()
        dkT[...] = jnp.zeros_like(dkT)
        dvT[...] = jnp.zeros_like(dvT)

        @pl.loop(0, 4)
        def _(qb):
            cols = mask_block(m, qb)

            @pl.loop(0, heads)
            def _(h):
                hrows = pl.ds(pl.multiple_of(h * HEAD_DIM, HEAD_DIM), HEAD_DIM)
                q = qT[m, hrows, cols]
                do = doT[hrows, cols]
                inner = jnp.sum(do.astype(F32) * oT[m, hrows, cols].astype(F32), axis=0, keepdims=True)
                log_total = lse[m, pl.ds(h, 1), cols]
                blank = jnp.zeros((HEAD_DIM, R), BF16)
                q_rhs = jnp.concatenate([q, blank], axis=0)
                do_rhs = jnp.concatenate([blank, do], axis=0)
                for c in range(L // KC):
                    rows = slice(c * KC, (c + 1) * KC)
                    s = mm(kv[m, h, rows, :], q_rhs) + bias_scr[rows, :]
                    p = jnp.exp(s - log_total)
                    dprob = mm(kv[m, h, rows, :], do_rhs)
                    p_scr[rows, :] = p.astype(BF16)
                    ds_scr[rows, :] = (p * (dprob - inner)).astype(BF16)
                dvT[hrows, :] += mm_nt(do, p_scr[...])
                dkT[hrows, :] += mm_nt(q, ds_scr[...])
                dqkvT[hrows, cols] = (mm(kT[m, hrows, :], ds_scr[...]) * scale).astype(BF16)

            for at, hook in hooks.items():
                pl.when(qb == at)(hook)

        dqkvT[HL : 2 * HL, :] = dkT[...].astype(BF16)
        dqkvT[2 * HL :, :] = dvT[...].astype(BF16)
        rs = rs_da[m]
        for r in (3, 2, 1, 0):
            part[micro + m, r] = mm_tn(dqkvT[:, r * R : (r + 1) * R], wq[...]).astype(BF16)
            if r == 3:
                rs.start_far()
            if r == 1:
                rs.start_near()
                rs.relay()

    def out_sums(m):
        B = min(256, D)

        @pl.loop(0, D // B)
        def _(i):
            f = pl.ds(pl.multiple_of(i * B, B), B)
            for r in range(4):
                o = mm_tt(d_all[m, r, :, f], oT[m, :, r * R : (r + 1) * R])
                if m == 0 and r == 0:
                    g_o[f, :] = o
                else:
                    g_o[f, :] += o

    def head_sums(m):
        B = min(256, D)
        sums = mm_nt(jnp.ones((8, L), BF16), dqkvT[...])[:1]
        if m == 0:
            qvb_ref[...] = sums
        else:
            qvb_ref[...] += sums

        @pl.loop(0, D // B)
        def _(i):
            f = pl.ds(pl.multiple_of(i * B, B), B)
            for r in range(4):
                j = mm_tt(a_all[m, r, :, f], dqkvT[:, r * R : (r + 1) * R])
                if m == 0 and r == 0:
                    g_j[f, :] = j
                else:
                    g_j[f, :] += j

    def finish_out(m):
        rs_branch[m].arrive()

        def step(rows):
            out_ref[m, rows, :] = (mid[m, rows, :] + (rs_branch[m].total(rows) + line(bias_down))).astype(BF16)

        by_rows(step)

    def finish_in(m):
        rs_da[m].arrive()

        def step(rows):
            da = rs_da[m].total(rows)
            n, r = norm_parts(x_ref[m, rows, :].astype(F32))
            add_row(0, da * n)
            add_row(1, da)
            gtok_ref[m, rows, :] += norm_back(da * line(gain1), n, r)

        by_rows(step)

    class Reduce:
        def __init__(self, acc, xs, xr, zr):
            self.acc, self.xs, self.xr, self.zr = acc, xs, xr, zr
            self.rows = D // n_dp
            self.n2 = n_dp // 2
            self.px = lax.rem(dp, 2)
            self.pz = dp // 2
            self.x = names.copy(xs, xr, {"dp": dp + 1 - 2 * self.px})
            self.z = []
            for off in range(1, self.n2):
                to = lax.rem(self.pz + off, self.n2)
                self.z.append(names.copy(xs.at[off - 1], zr.at[off - 1], {"dp": 2 * to + self.px}))

        def at(self, z, px):
            n = self.rows
            return pl.ds(pl.multiple_of((2 * z + px) * n, n), n)

        def start(self):
            for z in range(self.n2):
                self.xs[z] = self.acc[self.at(z, 1 - self.px), :].astype(BF16)
            self.x.start()

        def second(self):
            self.x.wait_send()
            self.x.wait_recv()
            for off in range(1, self.n2):
                to = lax.rem(self.pz + off, self.n2)
                self.xs[off - 1] = (self.acc[self.at(to, self.px), :] + self.xr[to].astype(F32)).astype(BF16)
                self.z[off - 1].start()

        def last(self):
            tot = self.acc[self.at(self.pz, self.px), :] + self.xr[self.pz].astype(F32)
            for off in range(1, self.n2):
                self.z[off - 1].wait_recv()
                tot = tot + self.zr[off - 1].astype(F32)
            return tot

        def drain(self):
            for c in self.z:
                c.wait_send()

    if in_dp:
        dn, up, ro, rj = (Reduce(acc, *stages[3 * i : 3 * i + 3]) for i, acc in enumerate((g_dn, g_up, g_o, g_j)))
        small_t = [names.copy(vec, trecv.at[i], {"tensor": d}) for i, d in enumerate((t_core, t_y, t_diag))]
        small_d = [names.copy(dsend, drecv.at[off - 1], {"dp": lax.rem(dp + off, n_dp)}) for off in range(1, n_dp)]

    def reduce(*steps):
        if in_dp:
            for step in steps:
                step()

    vec[...] = jnp.zeros_like(vec)
    first_norm(0)
    pl.semaphore_wait(barrier, met)
    ag_a[0].start_core()
    ag_a[0].start_y()
    for m in range(1, micro):
        first_norm(m)
        ag_a[m].start_core()
        ag_a[m].start_y()
    for ld in loads[4 + 2 * heads :]:
        ld.wait()
    for m in range(micro):
        ag_g[m].start_core()
    ag_g[0].start_y()
    codes(0)
    for ld in loads[:2] + loads[4 : 4 + 2 * heads]:
        ld.wait()

    qkv(0)
    attend(0)
    attn_out(0)
    codes(1)
    qkv(1)
    attend(1)
    attn_out(1)
    loads[2].wait()
    loads[3].wait()

    def feed_all(m, between, after):
        ag_c[m].wait_core()
        ag_g[m].wait_core()
        rs_attn[m].drain()
        feed(m, 0)
        rs_dc[m].start_near()
        rs_branch[m].start_near()
        between()
        ag_c[m].forward()
        ag_g[m].forward()
        ag_c[m].wait_last()
        ag_g[m].wait_last()
        feed(m, 2)
        rs_dc[m].start_far()
        rs_dc[m].relay()
        rs_branch[m].start_far()
        after()
        weight_sums(m)

    middle(0)
    feed_all(0, lambda: middle(1), lambda: ag_g[1].start_y())
    feed_all(1, lambda: turn(0), lambda: None)
    if in_dp:
        reduce(dn.start, up.start)

    def late_turn():
        turn(1)
        if in_dp:
            reduce(dn.second)

    codes(0)
    rs_dc[0].drain()
    attend_back(0, lambda: out_sums(0), {2: late_turn})
    rs_branch[0].relay()
    head_sums(0)
    codes(1)
    rs_dc[1].drain()

    def out_ready():
        out_sums(1)
        if in_dp:
            reduce(ro.start)

    def mid_back():
        if in_dp:
            reduce(up.second)

    def late_back():
        if in_dp:
            reduce(ro.second)

    attend_back(1, out_ready, {0: mid_back, 2: late_back})
    rs_branch[1].relay()
    head_sums(1)
    if in_dp:
        rj.start()
    finish_in(0)
    finish_out(0)
    if in_dp:
        own_dn[...] = dn.last()
        own_up[...] = up.last()
        own_o[...] = ro.last()
        rj.second()
    finish_in(1)
    if in_dp:
        vec[7:8, : 3 * HL] = qvb_ref[...]
        for c in small_t:
            c.start()
        for c in small_t:
            c.wait_recv()
        six = lax.broadcasted_iota(jnp.int32, vec.shape, 0) < 6
        dsend[...] = vec[...] + jnp.where(six, trecv[0] + trecv[1] + trecv[2], 0.0)
        for c in small_d:
            c.start()
    finish_out(1)
    if in_dp:
        tot = rj.last()
        for i in range(3):
            own_j[i] = tot[:, i * HL : (i + 1) * HL]
        tot = dsend[...]
        for i, c in enumerate(small_d):
            c.wait_recv()
            tot = tot + drecv[i]
        small_ref[...] = tot
        for c in small_t + small_d:
            c.wait_send()
        for r in (dn, up, ro, rj):
            r.drain()
    else:
        small_ref[...] = vec[...]
        own_dn[...] = g_dn[...]
        own_up[...] = g_up[...]
        own_o[...] = g_o[...]
        for i in range(3):
            own_j[i] = g_j[:, i * HL : (i + 1) * HL]
    for m in range(micro):
        rs_branch[m].drain()
        rs_da[m].drain()
        for gather in (ag_a, ag_c, ag_g, ag_d):
            gather[m].drain()


def body(
    n_dp,
    tokens,
    segment_ids,
    valid_mask,
    gain_one,
    shift_one,
    w_qkv,
    bias_qv,
    output_weight,
    bias_out,
    gain_two,
    shift_two,
    up_weight,
    bias_up,
    down_weight,
    bias_down,
    out_grad,
):
    micro, R, _, D = tokens.shape
    L = 4 * R
    HL = w_qkv.shape[2]
    FL = up_weight.shape[1]
    heads = HL // HEAD_DIM
    in_dp = n_dp > 1 and n_dp % 2 == 0 and D % n_dp == 0 and (D // n_dp) % 16 == 0
    n2, rows = n_dp // 2, D // n_dp
    wqT = jnp.transpose(w_qkv, (1, 2, 0)).reshape(3 * HL, D)
    vmem = pl.BlockSpec(memory_space=pltpu.VMEM)
    hbm = pl.BlockSpec(memory_space=pl.ANY)
    own_rows = rows if in_dp else D
    widths = (FL, FL, HL, 3 * HL)
    scratch = [
        pltpu.VMEM((3 * HL, D), BF16),
        pltpu.VMEM((2 * HL, D), BF16),
        pltpu.VMEM((HL, D), BF16),
        pltpu.VMEM((D, FL), BF16),
        pltpu.VMEM((FL, D), BF16),
        pltpu.VMEM((micro, 4, R, D), BF16),
        pltpu.VMEM((micro, 4, R, D), BF16),
        pltpu.VMEM((micro, 4, R, D), BF16),
        pltpu.VMEM((micro, 4, R, D), BF16),
        pltpu.VMEM((micro, HL, L), BF16),
        pltpu.VMEM((micro, HL, L), BF16),
        pltpu.VMEM((micro, HL, L), BF16),
        pltpu.VMEM((micro, heads, L, 2 * HEAD_DIM), BF16),
        pltpu.VMEM((micro, HL, L), BF16),
        pltpu.VMEM((micro, heads, L), F32),
        pltpu.VMEM((HL, L), BF16),
        pltpu.VMEM((L, FL), BF16),
        pltpu.VMEM((L, FL), BF16),
        pltpu.VMEM((L, 128), F32),
        pltpu.VMEM((L, R), F32),
        pltpu.VMEM((L, R), F32),
        pltpu.VMEM((L, R), BF16),
        pltpu.VMEM((L, R), BF16),
        pltpu.VMEM((HL, L), F32),
        pltpu.VMEM((HL, L), F32),
        pltpu.VMEM((3 * HL, L), BF16),
        pltpu.VMEM((2 * micro, 4, R, D), BF16),
        pltpu.VMEM((2 * micro, 2, R, D), BF16),
        pltpu.VMEM((2 * micro, R, D), BF16),
        pltpu.VMEM((2 * micro, R, D), BF16),
        pltpu.VMEM((micro, R, D), F32),
        *(pltpu.VMEM((D, c), F32) for c in widths),
    ]
    if in_dp:
        for c in widths:
            scratch += [
                pltpu.VMEM((n2, rows, c), BF16),
                pltpu.VMEM((n2, rows, c), BF16),
                pltpu.VMEM((n2 - 1, rows, c), BF16),
            ]
    scratch += [pltpu.VMEM((8, D), F32)]
    if in_dp:
        scratch += [pltpu.VMEM((3, 8, D), F32), pltpu.VMEM((8, D), F32), pltpu.VMEM((n_dp - 1, 8, D), F32)]
    scratch += [pltpu.SemaphoreType.DMA((SEMS,)), pltpu.SemaphoreType.DMA((SEMS,)), pltpu.SemaphoreType.DMA((6 + 2 * heads,))]
    outs = pl.pallas_call(
        functools.partial(block_kernel, n_dp, in_dp),
        out_shape=(
            jax.ShapeDtypeStruct((micro, R, D), BF16),
            jax.ShapeDtypeStruct((micro, R, D), F32),
            jax.ShapeDtypeStruct((8, D), F32),
            jax.ShapeDtypeStruct((1, 3 * HL), F32),
            jax.ShapeDtypeStruct((own_rows, FL), F32),
            jax.ShapeDtypeStruct((own_rows, FL), F32),
            jax.ShapeDtypeStruct((own_rows, HL), F32),
            jax.ShapeDtypeStruct((3, own_rows, HL), F32),
        ),
        in_specs=[vmem, hbm] + [vmem] * 10 + [hbm] * 4,
        out_specs=[vmem] * 8,
        scratch_shapes=scratch,
        compiler_params=pltpu.CompilerParams(
            collective_id=0, has_side_effects=True, vmem_limit_bytes=67043328
        ),
        name="vision_block",
    )(
        tokens.reshape(micro, R, D),
        out_grad.reshape(micro, R, D),
        segment_ids,
        valid_mask,
        gain_one,
        shift_one,
        bias_qv,
        bias_out,
        gain_two,
        shift_two,
        bias_up,
        bias_down,
        wqT,
        output_weight,
        up_weight,
        down_weight,
    )
    out, gtok, small, qvb, share_dn, share_up, share_o, share_j = outs
    if not in_dp:
        share_dn, share_up, share_o = (lax.psum_scatter(v, "dp", scatter_dimension=0, tiled=True) for v in (share_dn, share_up, share_o))
        share_j = lax.psum_scatter(share_j, "dp", scatter_dimension=1, tiled=True)
        small = jnp.concatenate([lax.psum(small[:6], ("dp", "tensor")), lax.psum(small[6:7], "dp")])
        sums = lax.psum(qvb[0], "dp")
    else:
        sums = small[7, : 3 * HL]
    grad_bias_qv = jnp.stack([sums[:HL], sums[2 * HL :]])
    return (
        out.reshape(micro, R, 1, D),
        gtok.reshape(micro, R, 1, D),
        small[0],
        small[1],
        jnp.transpose(share_j, (1, 0, 2)),
        grad_bias_qv,
        share_o.T,
        small[2],
        small[3],
        small[4],
        share_up,
        small[6, :FL],
        share_dn.T,
        small[5],
    )


def solution(mesh):
    placed = (
        P(None, "tensor", "dp", None),
        P(None, "dp", None),
        P(None, "dp", None),
        P(),
        P(),
        P(None, None, "tensor"),
        P(None, "tensor"),
        P("tensor", None),
        P(),
        P(),
        P(),
        P(None, "tensor"),
        P("tensor"),
        P("tensor", None),
        P(),
        P(None, "tensor", "dp", None),
    )
    return jax.shard_map(
        functools.partial(body, mesh.shape["dp"]),
        mesh=mesh,
        in_specs=placed,
        out_specs=(
            P(None, "tensor", "dp", None),
            P(None, "tensor", "dp", None),
            P(),
            P(),
            P("dp", None, "tensor"),
            P(None, "tensor"),
            P("tensor", "dp"),
            P(),
            P(),
            P(),
            P("dp", "tensor"),
            P("tensor"),
            P("tensor", "dp"),
            P(),
        ),
        check_vma=False,
    )
```

```python
import functools

import jax
import jax.numpy as jnp
from jax import lax
from jax.experimental import pallas as pl
from jax.experimental.pallas import tpu as pltpu
from jax.sharding import PartitionSpec as P

HEAD_DIM = 64
EPS = 1e-06
MASKED = -1e30
SELF_CODE = 4096.0
F32 = jnp.float32
BF16 = jnp.bfloat16
MESH = pl.DeviceIdType.MESH
GELU_A = 0.7978845608028654
GELU_B = 0.044715


def mm(a, b):
    return lax.dot_general(a, b, (((1,), (0,)), ((), ())), preferred_element_type=F32)


def mm_nt(a, b):
    return lax.dot_general(a, b, (((1,), (1,)), ((), ())), preferred_element_type=F32)


def mm_tn(a, b):
    return lax.dot_general(a, b, (((0,), (0,)), ((), ())), preferred_element_type=F32)


def mm_tt(a, b):
    return lax.dot_general(a, b, (((0,), (1,)), ((), ())), preferred_element_type=F32)


def norm_parts(v):
    mean = jnp.mean(v, axis=-1, keepdims=True)
    cen = v - mean
    r = lax.rsqrt(jnp.mean(cen * cen, axis=-1, keepdims=True) + EPS)
    return cen * r, r


def norm_back(e, n, r):
    first = jnp.mean(e, axis=-1, keepdims=True)
    second = jnp.mean(e * n, axis=-1, keepdims=True)
    return r * (e - first - n * second)


class Names:
    def __init__(self, send, recv):
        self.send, self.recv, self.used = send, recv, 0

    def copy(self, src, dst, device):
        i = self.used
        self.used += 1
        return pltpu.make_async_remote_copy(
            src_ref=src,
            dst_ref=dst,
            send_sem=self.send.at[i],
            recv_sem=self.recv.at[i],
            device_id=device,
            device_id_type=MESH,
        )


SEMS = 120


def block_kernel(
    n_dp,
    in_dp,
    x_ref,
    g_ref,
    seg_ref,
    val_ref,
    gain1,
    shift1,
    bias_qv,
    bias_out,
    gain2,
    shift2,
    bias_up,
    bias_down,
    wqkv_hbm,
    wo_hbm,
    wu_hbm,
    wd_hbm,
    out_ref,
    gtok_ref,
    small_ref,
    qvb_ref,
    own_dn,
    own_up,
    own_o,
    own_j,
    wq,
    wkv,
    wo,
    wu,
    wd,
    a_all,
    c_all,
    g_all,
    d_all,
    qT,
    kT,
    vT,
    kv,
    oT,
    lse,
    doT,
    h_scr,
    du_scr,
    kcol,
    bias_scr,
    s_scr,
    p_scr,
    ds_scr,
    dkT,
    dvT,
    dqkvT,
    part,
    crecv,
    ysend,
    yrecv,
    mid,
    g_dn,
    g_up,
    g_o,
    g_q,
    g_kv,
    *rest,
):
    if in_dp:
        stages, (vec, trecv, dsend, drecv, send_sem, recv_sem, w_sem) = rest[:15], rest[15:]
    else:
        vec, send_sem, recv_sem, w_sem = rest
    micro, R, D = x_ref.shape
    line = lambda ref: ref[...].reshape(1, -1)
    L = 4 * R
    HL = wo.shape[0]
    FL = wu.shape[1]
    heads = HL // HEAD_DIM
    scale = HEAD_DIM ** (-0.5)
    t = lax.axis_index("tensor")
    dp = lax.axis_index("dp")
    t_core = t + 1 - 2 * lax.rem(t, 2)
    t_y = lax.rem(t + 2, 4)
    t_diag = t_core + 2 - 4 * (t_core // 2)
    blocks = (t, t_core, t_y, t_diag)
    core = {"tensor": t_core}
    ydev = {"tensor": t_y}
    names = Names(send_sem, recv_sem)

    barrier = pltpu.get_barrier_semaphore()
    met = 0
    for dev in (t_core, t_y, t_diag):
        pl.semaphore_signal(barrier, inc=1, device_id={"tensor": dev}, device_id_type=MESH)
        met += 1
    if in_dp:
        for off in range(1, n_dp):
            pl.semaphore_signal(barrier, inc=1, device_id={"dp": lax.rem(dp + off, n_dp)}, device_id_type=MESH)
            met += 1
    loads = [
        pltpu.make_async_copy(s, d, w_sem.at[i])
        for i, (s, d) in enumerate(((wqkv_hbm, wq), (wo_hbm, wo), (wu_hbm, wu), (wd_hbm, wd)))
    ]
    for h in range(heads):
        for j in range(2):
            src = wqkv_hbm.at[pl.ds((1 + j) * HL + h * HEAD_DIM, HEAD_DIM), :]
            dst = wkv.at[pl.ds((2 * h + j) * HEAD_DIM, HEAD_DIM), :]
            loads.append(pltpu.make_async_copy(src, dst, w_sem.at[len(loads)]))
    for m in range(micro):
        loads.append(pltpu.make_async_copy(g_ref.at[m], g_all.at[m, 0], w_sem.at[len(loads)]))
    for ld in loads:
        ld.start()

    CH = min(64, R // 2)
    KC = min(128, R)

    half = R // 2

    class Gather:
        def __init__(self, buf, m):
            b = self.b = buf
            self.core = names.copy(b.at[m, 0], b.at[m, 1], core)
            self.y = [names.copy(b.at[m, 0, pl.ds(i * half, half)], b.at[m, 2, pl.ds(i * half, half)], ydev) for i in range(2)]
            self.fwd = [names.copy(b.at[m, 2, pl.ds(i * half, half)], b.at[m, 3, pl.ds(i * half, half)], core) for i in range(2)]

        def start_core(self):
            self.core.start()

        def start_y(self, *which):
            for i in which or (0, 1):
                self.y[i].start()

        def wait_core(self):
            self.core.wait_recv()

        def forward(self):
            for c, f in zip(self.y, self.fwd):
                c.wait_recv()
                f.start()

        def wait_last(self):
            for f in self.fwd:
                f.wait_recv()

        def drain(self):
            for c in [self.core] + self.y + self.fwd:
                c.wait_send()

    class Scatter:
        def __init__(self, p):
            self.p = p
            self.c3 = names.copy(part.at[p, 3], crecv.at[p, 1], core)
            self.c1 = names.copy(part.at[p, 1], crecv.at[p, 0], core)
            self.y = [names.copy(ysend.at[p, pl.ds(i * half, half)], yrecv.at[p, pl.ds(i * half, half)], ydev) for i in range(2)]
            self.met = False

        def start_far(self):
            self.c3.start()

        def start_near(self):
            self.c1.start()

        def relay(self, *which):
            p = self.p
            if not self.met:
                self.c3.wait_recv()
                self.met = True
            for i in which or (0, 1):

                @pl.loop(i * half // CH, (i + 1) * half // CH)
                def _(n):
                    rows = pl.ds(pl.multiple_of(n * CH, CH), CH)
                    ysend[p, rows, :] = (part[p, 2, rows, :].astype(F32) + crecv[p, 1, rows, :].astype(F32)).astype(BF16)

                self.y[i].start()

        def arrive(self):
            self.c1.wait_recv()
            for c in self.y:
                c.wait_recv()

        def total(self, rows):
            p = self.p
            return part[p, 0, rows, :].astype(F32) + crecv[p, 0, rows, :].astype(F32) + yrecv[p, rows, :].astype(F32)

        def drain(self):
            for c in [self.c3, self.c1] + self.y:
                c.wait_send()

    def by_rows(step):
        @pl.loop(0, R // CH)
        def _(i):
            step(pl.ds(pl.multiple_of(i * CH, CH), CH))

    ag_a = [Gather(a_all, m) for m in range(micro)]
    ag_c = [Gather(c_all, m) for m in range(micro)]
    ag_g = [Gather(g_all, m) for m in range(micro)]
    ag_d = [Gather(d_all, m) for m in range(micro)]
    rs_attn = [Scatter(m) for m in range(micro)]
    rs_branch = [Scatter(m) for m in range(micro)]
    rs_dc = [Scatter(micro + m) for m in range(micro)]
    rs_da = [Scatter(micro + m) for m in range(micro)]

    def first_norm(m):
        def step(rows):
            n, _ = norm_parts(x_ref[m, rows, :].astype(F32))
            a_all[m, 0, rows, :] = (n * line(gain1) + line(shift1)).astype(BF16)

        by_rows(step)

    def codes(m):
        for r in range(4):
            seg = seg_ref[m, :, pl.ds(pl.multiple_of(blocks[r] * R, R), R)].astype(F32)
            val = val_ref[m, :, pl.ds(pl.multiple_of(blocks[r] * R, R), R)]
            place = lax.broadcasted_iota(jnp.int32, (1, R), 1).astype(F32) + (SELF_CODE + r * R)
            code = jnp.where(val > 0, seg, place)
            kcol[pl.ds(r * R, R), :] = jnp.broadcast_to(code, (128, R)).T

    def qkv(m):
        cols_of = jnp.broadcast_to(bias_qv[...].reshape(2, 1, HL), (2, 8, HL))
        bq = cols_of[0].T[:, :1]
        bv = cols_of[1].T[:, :1]
        none = jnp.zeros((1, HEAD_DIM), F32)
        v_row = bias_qv[1:2, :]
        kv_bias = jnp.concatenate([p for h in range(heads) for p in (none, v_row[:, h * HEAD_DIM : (h + 1) * HEAD_DIM])], axis=1)

        def slot(r):
            a = a_all[m, r]
            cols = slice(r * R, (r + 1) * R)
            allT = mm_nt(wq[...], a)
            qT[m, :, cols] = (allT[:HL] + bq).astype(BF16) * jnp.asarray(scale, BF16)
            kT[m, :, cols] = allT[HL : 2 * HL].astype(BF16)
            vT[m, :, cols] = (allT[2 * HL :] + bv).astype(BF16)
            both = mm_nt(a, wkv[...]) + kv_bias
            for h in range(heads):
                kv[m, h, cols, :] = both[:, h * 128 : (h + 1) * 128].astype(BF16)

        slot(0)
        ag_a[m].wait_core()
        slot(1)
        ag_a[m].forward()
        slot(2)
        ag_a[m].wait_last()
        slot(3)

    def mask_block(m, qb):
        cols = pl.ds(pl.multiple_of(qb * R, R), R)
        place = (lax.broadcasted_iota(jnp.int32, (1, R), 1) + qb * R).astype(F32) + SELF_CODE
        blk = jnp.where(qb == 0, blocks[0], jnp.where(qb == 1, blocks[1], jnp.where(qb == 2, blocks[2], blocks[3])))
        seg = seg_ref[m, :, pl.ds(pl.multiple_of(blk * R, R), R)].astype(F32)
        for c in range(L // KC):
            kc = kcol[c * KC : (c + 1) * KC, :1]
            ok = (kc == seg) | (kc == place)
            bias_scr[c * KC : (c + 1) * KC, :] = jnp.where(ok, 0.0, MASKED)
        return cols

    def fold8(v, op):
        out = v[:8]
        for i in range(1, v.shape[0] // 8):
            out = op(out, v[i * 8 : (i + 1) * 8])
        return out

    def attend(m):
        @pl.loop(0, 4)
        def _(qb):
            cols = mask_block(m, qb)

            @pl.loop(0, heads)
            def _(h):
                hrows = pl.ds(pl.multiple_of(h * HEAD_DIM, HEAD_DIM), HEAD_DIM)
                q = jnp.concatenate([qT[m, hrows, cols], jnp.zeros((HEAD_DIM, R), BF16)], axis=0)
                top8 = None
                for c in range(L // KC):
                    rows = slice(c * KC, (c + 1) * KC)
                    s = mm(kv[m, h, rows, :], q) + bias_scr[rows, :]
                    s_scr[rows, :] = s
                    part8 = fold8(s, jnp.maximum)
                    top8 = part8 if top8 is None else jnp.maximum(top8, part8)
                top = jnp.max(top8, axis=0, keepdims=True)
                sum8 = None
                for c in range(L // KC):
                    rows = slice(c * KC, (c + 1) * KC)
                    p = jnp.exp(s_scr[rows, :] - top)
                    p_scr[rows, :] = p.astype(BF16)
                    part8 = fold8(p, jnp.add)
                    sum8 = part8 if sum8 is None else sum8 + part8
                total = jnp.sum(sum8, axis=0, keepdims=True)
                o = mm(vT[m, hrows, :], p_scr[...])
                oT[m, hrows, cols] = (o / total).astype(BF16)
                lse[m, pl.ds(h, 1), cols] = top + jnp.log(total)

    def attn_out(m):
        rs = rs_attn[m]
        for r in (3, 2, 1, 0):
            part[m, r] = mm_tn(oT[m, :, r * R : (r + 1) * R], wo[...]).astype(BF16)
            if r == 3:
                rs.start_far()
            if r == 1:
                rs.start_near()
        rs.relay()

    def middle(m):
        rs_attn[m].arrive()

        def step(rows):
            v = x_ref[m, rows, :].astype(F32) + (rs_attn[m].total(rows) + line(bias_out))
            mid[m, rows, :] = v
            n, _ = norm_parts(v)
            c_all[m, 0, rows, :] = (n * line(gain2) + line(shift2)).astype(BF16)

        by_rows(step)
        ag_c[m].start_core()
        ag_c[m].start_y()

    def feed(m, first, last_slot):
        @pl.loop(first, first + 2)
        def _(r):
            rows = pl.ds(pl.multiple_of(r * R, R), R)
            pl.when(r == 3)(last_slot)
            g = g_all[m, r]
            u = mm(c_all[m, r], wu[...]) + line(bias_up)
            dh = mm_nt(g, wd[...])
            th = jnp.tanh(GELU_A * (u + GELU_B * (u * u * u)))
            half_u = 0.5 * (1.0 + th)
            slope = half_u + (0.5 * u) * (1.0 - th * th) * (GELU_A * (1.0 + (3.0 * GELU_B) * (u * u)))
            hid = (u * half_u).astype(BF16)
            du = (dh * slope).astype(BF16)
            h_scr[rows, :] = hid
            du_scr[rows, :] = du
            vec[6:7, :FL] += jnp.sum(du.astype(F32), axis=0, keepdims=True)
            part[micro + m, r] = mm_nt(du, wu[...]).astype(BF16)
            part[m, r] = mm(hid, wd[...]).astype(BF16)

    def weight_sums(m):
        B = min(256, D)

        @pl.loop(0, D // B)
        def _(i):
            f = pl.ds(pl.multiple_of(i * B, B), B)
            for r in range(4):
                down = mm_tn(g_all[m, r, :, f], h_scr[r * R : (r + 1) * R, :])
                up = mm_tn(c_all[m, r, :, f], du_scr[r * R : (r + 1) * R, :])
                if m == 0 and r == 0:
                    g_dn[f, :] = down
                    g_up[f, :] = up
                else:
                    g_dn[f, :] += down
                    g_up[f, :] += up

    def add_row(i, v):
        vec[i : i + 1, :] += jnp.sum(v, axis=0, keepdims=True)

    def turn(m):
        rs_dc[m].arrive()

        def step(rows):
            dc = rs_dc[m].total(rows)
            n, r = norm_parts(mid[m, rows, :])
            add_row(3, dc * n)
            add_row(4, dc)
            g = g_all[m, 0, rows, :].astype(F32)
            add_row(5, g)
            dx = g + norm_back(dc * line(gain2), n, r)
            gtok_ref[m, rows, :] = dx
            low = dx.astype(BF16)
            add_row(2, low.astype(F32))
            d_all[m, 0, rows, :] = low

        by_rows(step)
        ag_d[m].start_core()
        ag_d[m].start_y()

    def attend_back(m, ready, hooks):
        def project(r):
            doT[:, r * R : (r + 1) * R] = mm_nt(wo[...], d_all[m, r]).astype(BF16)

        project(0)
        ag_d[m].wait_core()
        project(1)
        ag_d[m].forward()
        project(2)
        ag_d[m].wait_last()
        project(3)
        ready()
        dkT[...] = jnp.zeros_like(dkT)
        dvT[...] = jnp.zeros_like(dvT)

        @pl.loop(0, 4)
        def _(qb):
            cols = mask_block(m, qb)

            @pl.loop(0, heads)
            def _(h):
                hrows = pl.ds(pl.multiple_of(h * HEAD_DIM, HEAD_DIM), HEAD_DIM)
                q = qT[m, hrows, cols]
                do = doT[hrows, cols]
                inner = jnp.sum(do.astype(F32) * oT[m, hrows, cols].astype(F32), axis=0, keepdims=True)
                log_total = lse[m, pl.ds(h, 1), cols]
                blank = jnp.zeros((HEAD_DIM, R), BF16)
                q_rhs = jnp.concatenate([q, blank], axis=0)
                do_rhs = jnp.concatenate([blank, do], axis=0)
                for c in range(L // KC):
                    rows = slice(c * KC, (c + 1) * KC)
                    s = mm(kv[m, h, rows, :], q_rhs) + bias_scr[rows, :]
                    p = jnp.exp(s - log_total)
                    dprob = mm(kv[m, h, rows, :], do_rhs)
                    p_scr[rows, :] = p.astype(BF16)
                    ds_scr[rows, :] = (p * (dprob - inner)).astype(BF16)
                dvT[hrows, :] += mm_nt(do, p_scr[...])
                dkT[hrows, :] += mm_nt(q, ds_scr[...])
                dqkvT[hrows, cols] = (mm(kT[m, hrows, :], ds_scr[...]) * scale).astype(BF16)

            for at, hook in hooks.items():
                pl.when(qb == at)(hook)

        dqkvT[HL : 2 * HL, :] = dkT[...].astype(BF16)
        dqkvT[2 * HL :, :] = dvT[...].astype(BF16)
        rs = rs_da[m]
        for r in (3, 2, 1, 0):
            part[micro + m, r] = mm_tn(dqkvT[:, r * R : (r + 1) * R], wq[...]).astype(BF16)
            if r == 3:
                rs.start_far()
            if r == 1:
                rs.start_near()
        rs.relay()

    def out_sums(m):
        B = min(256, D)

        @pl.loop(0, D // B)
        def _(i):
            f = pl.ds(pl.multiple_of(i * B, B), B)
            for r in range(4):
                o = mm_tt(d_all[m, r, :, f], oT[m, :, r * R : (r + 1) * R])
                if m == 0 and r == 0:
                    g_o[f, :] = o
                else:
                    g_o[f, :] += o

    def head_sums(m, kv_done, q_done):
        B = min(256, D)
        sums = mm_nt(jnp.ones((8, L), BF16), dqkvT[...])[:1]
        if m == 0:
            qvb_ref[...] = sums
        else:
            qvb_ref[...] += sums

        for acc, lo, hi, done in ((g_kv, HL, 3 * HL, kv_done), (g_q, 0, HL, q_done)):

            @pl.loop(0, D // B)
            def _(i):
                f = pl.ds(pl.multiple_of(i * B, B), B)
                for r in range(4):
                    j = mm_tt(a_all[m, r, :, f], dqkvT[lo:hi, r * R : (r + 1) * R])
                    if m == 0 and r == 0:
                        acc[f, :] = j
                    else:
                        acc[f, :] += j

            done()

    def finish_out(m):
        rs_branch[m].arrive()

        def step(rows):
            out_ref[m, rows, :] = (mid[m, rows, :] + (rs_branch[m].total(rows) + line(bias_down))).astype(BF16)

        by_rows(step)

    def finish_in(m):
        rs_da[m].arrive()

        def step(rows):
            da = rs_da[m].total(rows)
            n, r = norm_parts(x_ref[m, rows, :].astype(F32))
            add_row(0, da * n)
            add_row(1, da)
            gtok_ref[m, rows, :] += norm_back(da * line(gain1), n, r)

        by_rows(step)

    class Reduce:
        def __init__(self, acc, xs, xr, zr):
            self.acc, self.xs, self.xr, self.zr = acc, xs, xr, zr
            self.rows = D // n_dp
            self.n2 = n_dp // 2
            self.px = lax.rem(dp, 2)
            self.pz = dp // 2
            self.x = names.copy(xs, xr, {"dp": dp + 1 - 2 * self.px})
            self.z = []
            for off in range(1, self.n2):
                to = lax.rem(self.pz + off, self.n2)
                self.z.append(names.copy(xs.at[off - 1], zr.at[off - 1], {"dp": 2 * to + self.px}))

        def at(self, z, px):
            n = self.rows
            return pl.ds(pl.multiple_of((2 * z + px) * n, n), n)

        def start(self):
            for z in range(self.n2):
                self.xs[z] = self.acc[self.at(z, 1 - self.px), :].astype(BF16)
            self.x.start()

        def second(self):
            self.x.wait_send()
            self.x.wait_recv()
            for off in range(1, self.n2):
                to = lax.rem(self.pz + off, self.n2)
                self.xs[off - 1] = (self.acc[self.at(to, self.px), :] + self.xr[to].astype(F32)).astype(BF16)
                self.z[off - 1].start()

        def last(self):
            tot = self.acc[self.at(self.pz, self.px), :] + self.xr[self.pz].astype(F32)
            for off in range(1, self.n2):
                self.z[off - 1].wait_recv()
                tot = tot + self.zr[off - 1].astype(F32)
            return tot

        def drain(self):
            for c in self.z:
                c.wait_send()

    if in_dp:
        dn, up, ro, rq, rkv = (Reduce(acc, *stages[3 * i : 3 * i + 3]) for i, acc in enumerate((g_dn, g_up, g_o, g_q, g_kv)))
        small_t = [names.copy(vec, trecv.at[i], {"tensor": d}) for i, d in enumerate((t_core, t_y, t_diag))]
        small_d = [names.copy(dsend, drecv.at[off - 1], {"dp": lax.rem(dp + off, n_dp)}) for off in range(1, n_dp)]

    def reduce(*steps):
        if in_dp:
            for step in steps:
                step()

    vec[...] = jnp.zeros_like(vec)
    first_norm(0)
    pl.semaphore_wait(barrier, met)
    ag_a[0].start_core()
    ag_a[0].start_y()
    for m in range(1, micro):
        first_norm(m)
        ag_a[m].start_core()
        ag_a[m].start_y()
    for ld in loads[4 + 2 * heads :]:
        ld.wait()
    for m in range(micro):
        ag_g[m].start_core()
    ag_g[0].start_y()
    ag_g[1].start_y(0)
    codes(0)
    for ld in loads[:2] + loads[4 : 4 + 2 * heads]:
        ld.wait()

    qkv(0)
    attend(0)
    attn_out(0)
    ag_g[1].start_y(1)
    codes(1)
    qkv(1)
    attend(1)
    attn_out(1)
    loads[2].wait()
    loads[3].wait()

    def feed_all(m, between, after):
        ag_c[m].wait_core()
        ag_g[m].wait_core()
        rs_attn[m].drain()
        feed(m, 0, lambda: None)
        rs_dc[m].start_near()
        rs_branch[m].start_near()
        between()
        ag_c[m].forward()
        ag_g[m].forward()

        def last_slot():
            ag_c[m].wait_last()
            ag_g[m].wait_last()

        feed(m, 2, last_slot)
        rs_dc[m].start_far()
        rs_dc[m].relay()
        rs_branch[m].start_far()
        after()
        weight_sums(m)

    middle(0)
    feed_all(0, lambda: middle(1), lambda: None)
    feed_all(1, lambda: turn(0), lambda: rs_branch[0].relay(0))
    if in_dp:
        reduce(dn.start, up.start)

    def late_turn():
        turn(1)
        if in_dp:
            reduce(dn.second)

    codes(0)
    rs_dc[0].drain()
    attend_back(0, lambda: out_sums(0), {2: late_turn})
    rs_branch[0].relay(1)
    rs_branch[1].relay(0)
    head_sums(0, lambda: None, lambda: None)
    codes(1)
    rs_dc[1].drain()

    def out_ready():
        out_sums(1)
        if in_dp:
            reduce(ro.start)

    def mid_back():
        if in_dp:
            reduce(up.second)

    def late_back():
        if in_dp:
            reduce(ro.second)

    attend_back(1, out_ready, {0: mid_back, 2: late_back})
    if in_dp:
        head_sums(1, rkv.start, rq.start)
    else:
        head_sums(1, lambda: None, lambda: None)
    finish_in(0)
    finish_out(0)
    if in_dp:
        own_dn[...] = dn.last()
        own_up[...] = up.last()
        own_o[...] = ro.last()
        rkv.second()
        rq.second()
    finish_in(1)
    if in_dp:
        vec[7:8, : 3 * HL] = qvb_ref[...]
        for c in small_t:
            c.start()
    rs_branch[1].relay(1)
    if in_dp:
        for c in small_t:
            c.wait_recv()
        six = lax.broadcasted_iota(jnp.int32, vec.shape, 0) < 6
        dsend[...] = vec[...] + jnp.where(six, trecv[0] + trecv[1] + trecv[2], 0.0)
        for c in small_d:
            c.start()
    finish_out(1)
    if in_dp:
        tot = rkv.last()
        own_j[1] = tot[:, :HL]
        own_j[2] = tot[:, HL:]
        own_j[0] = rq.last()
        tot = dsend[...]
        for i, c in enumerate(small_d):
            c.wait_recv()
            tot = tot + drecv[i]
        small_ref[...] = tot
        for c in small_t + small_d:
            c.wait_send()
        for r in (dn, up, ro, rq, rkv):
            r.drain()
    else:
        small_ref[...] = vec[...]
        own_dn[...] = g_dn[...]
        own_up[...] = g_up[...]
        own_o[...] = g_o[...]
        own_j[0] = g_q[...]
        own_j[1] = g_kv[:, :HL]
        own_j[2] = g_kv[:, HL:]
    for m in range(micro):
        rs_branch[m].drain()
        rs_da[m].drain()
        for gather in (ag_a, ag_c, ag_g, ag_d):
            gather[m].drain()


def body(
    n_dp,
    tokens,
    segment_ids,
    valid_mask,
    gain_one,
    shift_one,
    w_qkv,
    bias_qv,
    output_weight,
    bias_out,
    gain_two,
    shift_two,
    up_weight,
    bias_up,
    down_weight,
    bias_down,
    out_grad,
):
    micro, R, _, D = tokens.shape
    L = 4 * R
    HL = w_qkv.shape[2]
    FL = up_weight.shape[1]
    heads = HL // HEAD_DIM
    in_dp = n_dp > 1 and n_dp % 2 == 0 and D % n_dp == 0 and (D // n_dp) % 16 == 0
    n2, rows = n_dp // 2, D // n_dp
    wqT = jnp.transpose(w_qkv, (1, 2, 0)).reshape(3 * HL, D)
    vmem = pl.BlockSpec(memory_space=pltpu.VMEM)
    hbm = pl.BlockSpec(memory_space=pl.ANY)
    own_rows = rows if in_dp else D
    widths = (FL, FL, HL, HL, 2 * HL)
    scratch = [
        pltpu.VMEM((3 * HL, D), BF16),
        pltpu.VMEM((2 * HL, D), BF16),
        pltpu.VMEM((HL, D), BF16),
        pltpu.VMEM((D, FL), BF16),
        pltpu.VMEM((FL, D), BF16),
        pltpu.VMEM((micro, 4, R, D), BF16),
        pltpu.VMEM((micro, 4, R, D), BF16),
        pltpu.VMEM((micro, 4, R, D), BF16),
        pltpu.VMEM((micro, 4, R, D), BF16),
        pltpu.VMEM((micro, HL, L), BF16),
        pltpu.VMEM((micro, HL, L), BF16),
        pltpu.VMEM((micro, HL, L), BF16),
        pltpu.VMEM((micro, heads, L, 2 * HEAD_DIM), BF16),
        pltpu.VMEM((micro, HL, L), BF16),
        pltpu.VMEM((micro, heads, L), F32),
        pltpu.VMEM((HL, L), BF16),
        pltpu.VMEM((L, FL), BF16),
        pltpu.VMEM((L, FL), BF16),
        pltpu.VMEM((L, 128), F32),
        pltpu.VMEM((L, R), F32),
        pltpu.VMEM((L, R), F32),
        pltpu.VMEM((L, R), BF16),
        pltpu.VMEM((L, R), BF16),
        pltpu.VMEM((HL, L), F32),
        pltpu.VMEM((HL, L), F32),
        pltpu.VMEM((3 * HL, L), BF16),
        pltpu.VMEM((2 * micro, 4, R, D), BF16),
        pltpu.VMEM((2 * micro, 2, R, D), BF16),
        pltpu.VMEM((2 * micro, R, D), BF16),
        pltpu.VMEM((2 * micro, R, D), BF16),
        pltpu.VMEM((micro, R, D), F32),
        *(pltpu.VMEM((D, c), F32) for c in widths),
    ]
    if in_dp:
        for c in widths:
            scratch += [
                pltpu.VMEM((n2, rows, c), BF16),
                pltpu.VMEM((n2, rows, c), BF16),
                pltpu.VMEM((n2 - 1, rows, c), BF16),
            ]
    scratch += [pltpu.VMEM((8, D), F32)]
    if in_dp:
        scratch += [pltpu.VMEM((3, 8, D), F32), pltpu.VMEM((8, D), F32), pltpu.VMEM((n_dp - 1, 8, D), F32)]
    scratch += [pltpu.SemaphoreType.DMA((SEMS,)), pltpu.SemaphoreType.DMA((SEMS,)), pltpu.SemaphoreType.DMA((6 + 2 * heads,))]
    outs = pl.pallas_call(
        functools.partial(block_kernel, n_dp, in_dp),
        out_shape=(
            jax.ShapeDtypeStruct((micro, R, D), BF16),
            jax.ShapeDtypeStruct((micro, R, D), F32),
            jax.ShapeDtypeStruct((8, D), F32),
            jax.ShapeDtypeStruct((1, 3 * HL), F32),
            jax.ShapeDtypeStruct((own_rows, FL), F32),
            jax.ShapeDtypeStruct((own_rows, FL), F32),
            jax.ShapeDtypeStruct((own_rows, HL), F32),
            jax.ShapeDtypeStruct((3, own_rows, HL), F32),
        ),
        in_specs=[vmem, hbm] + [vmem] * 10 + [hbm] * 4,
        out_specs=[vmem] * 8,
        scratch_shapes=scratch,
        compiler_params=pltpu.CompilerParams(
            collective_id=0, has_side_effects=True, vmem_limit_bytes=67043328
        ),
        name="vision_block",
    )(
        tokens.reshape(micro, R, D),
        out_grad.reshape(micro, R, D),
        segment_ids,
        valid_mask,
        gain_one,
        shift_one,
        bias_qv,
        bias_out,
        gain_two,
        shift_two,
        bias_up,
        bias_down,
        wqT,
        output_weight,
        up_weight,
        down_weight,
    )
    out, gtok, small, qvb, share_dn, share_up, share_o, share_j = outs
    if not in_dp:
        share_dn, share_up, share_o = (lax.psum_scatter(v, "dp", scatter_dimension=0, tiled=True) for v in (share_dn, share_up, share_o))
        share_j = lax.psum_scatter(share_j, "dp", scatter_dimension=1, tiled=True)
        small = jnp.concatenate([lax.psum(small[:6], ("dp", "tensor")), lax.psum(small[6:7], "dp")])
        sums = lax.psum(qvb[0], "dp")
    else:
        sums = small[7, : 3 * HL]
    grad_bias_qv = jnp.stack([sums[:HL], sums[2 * HL :]])
    return (
        out.reshape(micro, R, 1, D),
        gtok.reshape(micro, R, 1, D),
        small[0],
        small[1],
        jnp.transpose(share_j, (1, 0, 2)),
        grad_bias_qv,
        share_o.T,
        small[2],
        small[3],
        small[4],
        share_up,
        small[6, :FL],
        share_dn.T,
        small[5],
    )


def solution(mesh):
    placed = (
        P(None, "tensor", "dp", None),
        P(None, "dp", None),
        P(None, "dp", None),
        P(),
        P(),
        P(None, None, "tensor"),
        P(None, "tensor"),
        P("tensor", None),
        P(),
        P(),
        P(),
        P(None, "tensor"),
        P("tensor"),
        P("tensor", None),
        P(),
        P(None, "tensor", "dp", None),
    )
    return jax.shard_map(
        functools.partial(body, mesh.shape["dp"]),
        mesh=mesh,
        in_specs=placed,
        out_specs=(
            P(None, "tensor", "dp", None),
            P(None, "tensor", "dp", None),
            P(),
            P(),
            P("dp", None, "tensor"),
            P(None, "tensor"),
            P("tensor", "dp"),
            P(),
            P(),
            P(),
            P("dp", "tensor"),
            P("tensor"),
            P("tensor", "dp"),
            P(),
        ),
        check_vma=False,
    )
```
